128 devices in a mesh: gx: 8 (over y, core), gy: 16 (over x, z).
Axes of the slice: x: 4, y: 4, z: 4, core: 2. Of those that a mesh axis runs over, the one named last changes fastest.
Arguments:
- child_value: bfloat16 [2097152, 128], P(('gx', 'gy')), may hold values from -6 to 6
- child_row: int32 [128, 16384], P(('gx', 'gy')), may hold values from 0 to 16383, each once within a row
- opp_set: int32 [2097152], P(('gx', 'gy')), may hold values from 0 to 262143, as said below
- opp_home: int32 [262144], replicated, may hold values from 0 to 262143, as said below
- opp_cum: float32 [262144, 128], P(('gx', 'gy')), may hold values from 0.01 to 1
- reach: float32 [16384], P(('gx', 'gy')), may hold values from 0.05 to 1
- br_set: int32 [16384], P(('gx', 'gy')), may hold values from 0 to 8191, as said below
- br_home: int32 [8192], replicated, may hold values from 0 to 8191, as said below
- br_cum: float32 [8192, 128], P(('gx', 'gy')), may hold values from 0.01 to 1
Outputs:
- history_value: float32 [2097152], P(('gx', 'gy'))
- regret_gap: float32 [8192], P(('gx', 'gy'))
- exploitability: float32 [], replicated
The draws below stay inside these ranges and needn't reach their ends.
Inputs may be any that keep to these rules, and one draw needn't show every extreme that they name: A permutation: opponent infoset i lives in row opp_home[i], owned by device opp_home[i] // 2048. `opp_set`: among the 16384 rows of one device at most 256 have infosets owned by any one device; in every draw some owner has exactly 256 from every device. A permutation: best-responder infoset i lives in row br_home[i], owned by device br_home[i] // 64. `br_set`: among the 128 rows of one device at most 2 have infosets owned by any one device; in every draw some owner has exactly 2 from every device.
All inputs are finite; a program needn't handle non-finite values.
Results may differ from the reference program's by a relative error of at most 0.0029.
Values may be sent and summed in bfloat16 or wider, within the bound.
A program may use at most 128 MiB of HBM per device.

```python
import math
import jax
import jax.numpy as jnp
from jax import lax

ACTIONS = 128
PAR_DEV = 128
S1_DEV = 2048
S2_DEV = 64
DEV_ALL = 128
HIST_DEV = 16384
HIST = 2097152
PARENTS = 16384
OPP_SETS = 262144
BR_SETS = 8192
CAP = 256
CAP2 = 2


def owner_table(key, count, salt):
    return jax.random.permutation(jax.random.fold_in(key, salt), count).astype(jnp.int32)


def pick_sets(key, home, per_owner, rows, limit, devices, salt):
    inverse = jnp.zeros_like(home).at[home].set(jnp.arange(home.shape[0], dtype=jnp.int32))
    favored = jax.random.randint(jax.random.fold_in(key, salt), (), 0, devices)

    def one_device(index):
        sub = jax.random.fold_in(jax.random.fold_in(key, salt + 1), index)
        scores = jax.random.permutation(sub, devices * limit).astype(jnp.int32)
        slots = jnp.arange(devices * limit, dtype=jnp.int32)
        scores = jnp.where(slots // limit == favored, scores - devices * limit, scores)
        order = jnp.argsort(scores, stable=True)[:rows]
        order = order[jax.random.permutation(jax.random.fold_in(sub, 5), rows)]
        owners = (order // limit).astype(jnp.int32)
        local = jax.random.randint(jax.random.fold_in(sub, 7), (rows,), 0, per_owner)
        return inverse[owners * per_owner + local]
    return jax.vmap(one_device)(jnp.arange(devices, dtype=jnp.int32)).reshape(-1)


def draw_opp_home(key, part):
    return owner_table(key, OPP_SETS, 101)


def draw_opp_set(key, part):
    home = owner_table(key, OPP_SETS, 101)
    return pick_sets(key, home, S1_DEV, HIST_DEV, CAP, DEV_ALL, 211)


def draw_br_home(key, part):
    return owner_table(key, BR_SETS, 307)


def draw_br_set(key, part):
    home = owner_table(key, BR_SETS, 307)
    return pick_sets(key, home, S2_DEV, PAR_DEV, CAP2, DEV_ALL, 409)


def level_of(stream_key, extent, pieces, smallest, high):
    level = 1.0
    for axis_at, shards_of in pieces:
        draws = jax.random.uniform(jax.random.fold_in(jax.random.fold_in(stream_key, 6), axis_at), (shards_of,), jnp.float32, smallest / len(pieces), high / len(pieces))
        level = level * jnp.repeat(jnp.exp(draws), extent[axis_at] // shards_of).reshape((-1,) + (1,) * (len(extent) - 1 - axis_at))
    return level


def scatter_about(rng, dims, scale, most, split=(), kind=jnp.bfloat16):
    gain = level_of(rng, dims, split, -0.22, 0.18) if split else 1.0
    result = jax.random.normal(rng, dims, jnp.float32) * scale * gain
    return jnp.minimum(jnp.maximum(result, -most), most).astype(kind)


def setup_inputs(seed: int = 0) -> dict:
    seeds = jax.random.split(jax.random.key(seed), 10)
    return {
        "child_value": scatter_about(seeds[0], (HIST, ACTIONS), 1.0, 6.0, ((0, 128),)),
        "child_row": jax.vmap(lambda own: jax.random.permutation(own, HIST_DEV))(jax.random.split(seeds[1], DEV_ALL)).reshape((DEV_ALL, HIST_DEV)).astype(jnp.int32),
        "opp_set": draw_opp_set(jax.random.fold_in(seeds[9], 71), 0),
        "opp_home": draw_opp_home(jax.random.fold_in(seeds[9], 71), 0),
        "opp_cum": jnp.clip(jnp.exp(math.log(1.0) - 4.6051702 * jax.random.uniform(seeds[4], (OPP_SETS, ACTIONS), jnp.float32) ** level_of(seeds[4], (OPP_SETS, ACTIONS), ((0, 128),), -0.2, 0.2)), 0.01, 1.0),
        "reach": jnp.clip(jnp.exp(math.log(1.0) - 2.9957323 * jax.random.uniform(seeds[5], (PARENTS,), jnp.float32) ** level_of(seeds[5], (PARENTS,), ((0, 128),), -0.2, 0.2)), 0.05, 1.0),
        "br_set": draw_br_set(jax.random.fold_in(seeds[9], 71), 0),
        "br_home": draw_br_home(jax.random.fold_in(seeds[9], 71), 0),
        "br_cum": jnp.clip(jnp.exp(math.log(1.0) - 4.6051702 * jax.random.uniform(seeds[8], (BR_SETS, ACTIONS), jnp.float32) ** level_of(seeds[8], (BR_SETS, ACTIONS), ((0, 128),), -0.2, 0.2)), 0.01, 1.0),
    }


def reference(child_value, child_row, opp_set, opp_home, opp_cum, reach, br_set, br_home, br_cum):
    policy = (opp_cum / jnp.sum(opp_cum, axis=1, keepdims=True)).astype(jnp.bfloat16)
    values = child_value.reshape(DEV_ALL, HIST_DEV, ACTIONS)
    sets = opp_set.reshape(DEV_ALL, HIST_DEV)

    def one_device(item):
        vals, ids, order = item
        rows = policy[opp_home[ids]]
        expect = jnp.sum(rows.astype(jnp.float32) * vals.astype(jnp.float32), axis=1)
        return expect, expect[order]

    expect, chosen = lax.map(one_device, (values, sets, child_row))
    history_value = expect.reshape(HIST)
    weighted = reach[:, None] * chosen.reshape(PARENTS, ACTIONS)
    action_value = jnp.zeros((BR_SETS, ACTIONS), jnp.float32).at[br_home[br_set]].add(weighted)
    br_policy = br_cum / jnp.sum(br_cum, axis=1, keepdims=True)
    regret_gap = jnp.max(action_value, axis=1) - jnp.sum(br_policy * action_value, axis=1)
    exploitability = jnp.sum(regret_gap) / jnp.sum(reach)
    return history_value, regret_gap, exploitability
```

```python
import functools

import jax
import jax.numpy as jnp
from jax import lax
from jax.experimental import pallas as pl
from jax.experimental.pallas import tpu as pltpu
from jax.sharding import Mesh
from jax.sharding import PartitionSpec as P

AXES = ("gx_0", "gx_1", "gy_0", "gy_1")
F32, BF16, I32 = jnp.float32, jnp.bfloat16, jnp.int32
NT = (((1,), (1,)), ((), ()))


def rows_iota(rows, cols):
    return lax.broadcasted_iota(I32, (rows, cols), 0)


def lanes_iota(rows, cols):
    return lax.broadcasted_iota(I32, (rows, cols), 1)


def dot(a, b):
    return jnp.dot(a, b, preferred_element_type=F32)


def one_hot_rows(rows, index):
    return (rows_iota(rows, index.shape[1]) == index).astype(F32).astype(BF16)


def pick(table, index, base=0):
    rows, n = table.shape
    mark = rows_iota(rows, n) == index
    return jnp.sum(jnp.where(mark, table, 0.0), axis=0, keepdims=True)


BLOCK = 8


def route_kernel(set_ref, home_ref, set2_ref, home2_ref,
                 want_ref, place_ref, want2_ref, place2_ref,
                 table, acc, carry):
    devices, slots = want_ref.shape
    home = home_ref[...]
    table[0:128, :] = ((home >> 9) - 256).astype(F32).T.astype(BF16)
    table[128:256, :] = ((home & 511) - 256).astype(F32).T.astype(BF16)
    acc[...] = jnp.zeros_like(acc)
    carry[...] = jnp.zeros_like(carry)
    upper = jnp.concatenate(
        [(rows_iota(128, 128) < lanes_iota(128, 128)).astype(F32), jnp.ones((128, 128), F32)], axis=1
    ).astype(BF16)

    def block(b, _):
        at = pl.ds(pl.multiple_of(b * BLOCK, BLOCK), BLOCK)
        index = set_ref[at, :]
        high, low = index >> 7, index & 127
        found = jnp.zeros((256, BLOCK * 128), F32)
        for c in range(table.shape[1] // 256):
            marks = jnp.concatenate(
                [one_hot_rows(256, high[j : j + 1, :] - 256 * c) for j in range(BLOCK)], axis=1
            )
            found += dot(table[:, 256 * c : 256 * (c + 1)], marks)
        members, values = [], []
        for j in range(BLOCK):
            lanes = slice(128 * j, 128 * (j + 1))
            mine = low[j : j + 1, :]
            top = pick(found[0:128, lanes], mine).astype(I32) + 256
            bottom = pick(found[128:256, lanes], mine).astype(I32) + 256
            row = (top << 9) + bottom
            owner, local = row >> 11, row & 2047
            member = rows_iota(128, 128) == owner
            member16 = member.astype(F32).astype(BF16)
            ahead = dot(member16, upper)
            rank = jnp.sum(
                jnp.where(member, ahead[:, :128] + carry[...], 0.0), axis=0, keepdims=True
            ).astype(I32)
            carry[...] += ahead[:, 128:]
            place_ref[pl.ds(b * BLOCK + j, 1), :] = owner * slots + rank
            mark = rows_iota(slots, 128) == rank
            values.append(
                jnp.concatenate(
                    [
                        jnp.where(mark, (local >> 6).astype(F32), 0.0),
                        jnp.where(mark, (local & 63).astype(F32), 0.0),
                    ],
                    axis=0,
                ).astype(BF16)
            )
            members.append(member16)
        acc[...] += lax.dot_general(
            jnp.concatenate(members, axis=1),
            jnp.concatenate(values, axis=1),
            NT,
            preferred_element_type=F32,
        )
        return 0

    lax.fori_loop(0, set_ref.shape[0] // BLOCK, block, 0)
    total = acc[...]
    want_ref[...] = (total[:, :slots] * 64.0 + total[:, slots:]).astype(I32)

    index2 = set2_ref[...]
    home2 = home2_ref[...]
    marks2 = one_hot_rows(home2.shape[0], index2 >> 7)
    top2 = dot((home2 >> 7).astype(F32).T.astype(BF16), marks2)
    bottom2 = dot((home2 & 127).astype(F32).T.astype(BF16), marks2)
    mine2 = index2 & 127
    row2 = pick(top2, mine2).astype(I32) * 128 + pick(bottom2, mine2).astype(I32)
    owner2, local2 = row2 >> 6, row2 & 63
    member2 = rows_iota(128, 128) == owner2
    ahead2 = dot(member2.astype(F32).astype(BF16), upper)
    rank2 = jnp.sum(jnp.where(member2, ahead2[:, :128], 0.0), axis=0, keepdims=True).astype(I32)
    place2_ref[...] = owner2 * 2 + rank2
    value2 = jnp.where(rows_iota(128, 128) == rank2, (local2 + 1).astype(F32), 0.0).astype(BF16)
    want2_ref[...] = lax.dot_general(
        member2.astype(F32).astype(BF16), value2, NT, preferred_element_type=F32
    ).astype(I32) - 1


def route(opp_set, opp_home, br_set, br_home, devices, slots):
    hist = opp_set.shape[0]
    return pl.pallas_call(
        route_kernel,
        out_shape=(
            jax.ShapeDtypeStruct((devices, slots), I32),
            jax.ShapeDtypeStruct((hist // 128, 128), I32),
            jax.ShapeDtypeStruct((devices, 128), I32),
            jax.ShapeDtypeStruct((1, 128), I32),
        ),
        scratch_shapes=[
            pltpu.VMEM((256, opp_home.shape[0] // 128), BF16),
            pltpu.VMEM((devices, 2 * slots), F32),
            pltpu.VMEM((devices, 128), F32),
        ],
        name="route",
    )(
        opp_set.reshape(-1, 128),
        opp_home.reshape(-1, 128),
        br_set.reshape(1, -1),
        br_home.reshape(-1, 128),
    )


def serve_kernel(asked_ref, cum_ref, out_ref, table):
    step = pl.program_id(0)
    half = table.shape[0]

    @pl.when(step == 0)
    def _():
        for part in range(2):
            cum = cum_ref[part * half : (part + 1) * half, :]
            policy = cum / jnp.sum(cum, axis=1, keepdims=True)
            table[:, 128 * part : 128 * (part + 1)] = policy.astype(BF16)

    for j in range(out_ref.shape[0]):
        device = step * out_ref.shape[0] + j
        column = jnp.sum(
            jnp.where(lanes_iota(*asked_ref.shape) == device, asked_ref[...], 0), axis=1, keepdims=True
        )
        slots = column.shape[0]
        row = column & (half - 1)
        marks = (lanes_iota(slots, half) == row).astype(F32).astype(BF16)
        both = dot(marks, table[...])
        out_ref[j] = jnp.where(column >= half, both[:, 128:], both[:, :128]).astype(BF16)


def serve(asked, opp_cum):
    devices, slots = asked.shape
    rows, acts = opp_cum.shape
    each = 8
    return pl.pallas_call(
        serve_kernel,
        grid=(devices // each,),
        in_specs=[
            pl.BlockSpec((slots, devices), lambda i: (0, 0)),
            pl.BlockSpec((rows, acts), lambda i: (0, 0)),
        ],
        out_specs=pl.BlockSpec((each, slots, acts), lambda i: (i, 0, 0)),
        out_shape=jax.ShapeDtypeStruct((devices, slots, acts), BF16),
        scratch_shapes=[pltpu.VMEM((rows // 2, 2 * acts), BF16)],
        name="serve",
    )(asked.T, opp_cum)


def arrange_kernel(place_ref, value_ref, out_ref, wide, slotted):
    hist = value_ref.shape[0]
    slotted[...] = jnp.zeros_like(slotted)
    wide[...] = value_ref[...].astype(F32)

    def some(b, _):
        for j in range(16):
            h = b * 16 + j
            slotted[pl.ds(place_ref[h], 1), :] = wide[pl.ds(h, 1), :]
        return 0

    lax.fori_loop(0, hist // 16, some, 0)
    out_ref[...] = slotted[...].astype(BF16)


def arrange(place, child_value, total):
    hist, acts = child_value.shape
    return pl.pallas_call(
        arrange_kernel,
        in_specs=[pl.BlockSpec(memory_space=pltpu.SMEM), pl.BlockSpec(memory_space=pltpu.VMEM)],
        out_shape=jax.ShapeDtypeStruct((total, acts), BF16),
        scratch_shapes=[pltpu.VMEM((hist, acts), F32), pltpu.VMEM((total, acts), F32)],
        cost_estimate=pl.CostEstimate(flops=0, transcendentals=0, bytes_accessed=200_000_000),
        name="arrange",
    )(place, child_value)


def split(x):
    high = x.astype(BF16)
    return high, (x - high.astype(F32)).astype(BF16)


def value_kernel(fetched_ref, child_ref, place_ref, next_ref, reach_ref, place2_ref,
                 value_ref, out_ref, table):
    step = pl.program_id(0)
    each, slots, acts = fetched_ref.shape

    @pl.when(step == 0)
    def _():
        table[...] = jnp.zeros_like(table)

    for j in range(each):
        product = fetched_ref[j].astype(F32) * child_ref[j].astype(F32)
        total = jnp.sum(product, axis=1, keepdims=True)
        table[...] = jnp.where(lanes_iota(slots, 128) == step * each + j, total, table[...])

    @pl.when(step == pl.num_programs(0) - 1)
    def _():
        pieces = jnp.concatenate(split(table[...]), axis=0)

        def history(b, _):
            at = pl.ds(pl.multiple_of(b * BLOCK, BLOCK), BLOCK)
            place = place_ref[at, :]
            owner, rank = place >> 8, place & 255
            marks = jnp.concatenate(
                [one_hot_rows(128, owner[j : j + 1, :]) for j in range(BLOCK)], axis=1
            )
            found = dot(pieces, marks)
            both = found[:slots, :] + found[slots:, :]
            for j in range(BLOCK):
                value_ref[pl.ds(b * BLOCK + j, 1), :] = pick(
                    both[:, 128 * j : 128 * (j + 1)], rank[j : j + 1, :]
                )
            return 0

        lax.fori_loop(0, place_ref.shape[0] // BLOCK, history, 0)
        values = jnp.concatenate(split(value_ref[...]), axis=0)

        def follow(b, _):
            at = pl.ds(pl.multiple_of(b * BLOCK, BLOCK), BLOCK)
            row = next_ref[at, :]
            marks = jnp.concatenate(
                [one_hot_rows(128, row[j : j + 1, :] & 127) for j in range(BLOCK)], axis=1
            )
            found = dot(values, marks)
            both = found[:128, :] + found[128:, :]
            for j in range(BLOCK):
                table[pl.ds(b * BLOCK + j, 1), :] = pick(
                    both[:, 128 * j : 128 * (j + 1)], row[j : j + 1, :] >> 7
                )
            return 0

        lax.fori_loop(0, next_ref.shape[0] // BLOCK, follow, 0)
        weighted = table[0:128, :] * reach_ref[...]
        marks2 = one_hot_rows(out_ref.shape[0], place2_ref[...])
        high, low = split(weighted)
        out_ref[...] = dot(marks2, high) + dot(marks2, low)


def values(fetched, arranged, place, child_row, reach, place2):
    devices, slots, acts = fetched.shape
    each = 8
    whole = lambda a: pl.BlockSpec(a.shape, lambda i: (0,) * a.ndim)
    block = pl.BlockSpec((each, slots, acts), lambda i: (i, 0, 0))
    rest = (place, child_row.reshape(-1, 128), reach.reshape(-1, 1), place2)
    return pl.pallas_call(
        value_kernel,
        grid=(devices // each,),
        in_specs=[block, block] + [whole(a) for a in rest],
        out_specs=(
            pl.BlockSpec(place.shape, lambda i: (0, 0)),
            pl.BlockSpec((2 * devices, acts), lambda i: (0, 0)),
        ),
        out_shape=(
            jax.ShapeDtypeStruct(place.shape, F32),
            jax.ShapeDtypeStruct((2 * devices, acts), F32),
        ),
        scratch_shapes=[pltpu.VMEM((slots, 128), F32)],
        name="values",
    )(fetched, arranged.reshape(fetched.shape), *rest)


def move(x):
    return lax.all_to_all(x, AXES, split_axis=0, concat_axis=0, tiled=True)


def local(child_value, child_row, opp_set, opp_home, opp_cum, reach, br_set, br_home, br_cum):
    devices = lax.axis_size(AXES)
    hist, acts = child_value.shape
    parents = reach.shape[0]
    slots = 2 * hist // devices
    want, place, want2, place2 = route(opp_set, opp_home, br_set, br_home, devices, slots)
    asked = move(jnp.concatenate([want, want2[:, :2]], axis=1))
    asked, asked2 = asked[:, :slots], asked[:, slots:].reshape(-1)
    served = serve(asked, opp_cum)
    fetched = move(served)
    arranged = arrange(place.reshape(-1), child_value, devices * slots)
    history_value, outgoing = values(fetched, arranged, place, child_row, reach, place2)
    incoming = move(outgoing.reshape(devices, 2, acts)).reshape(2 * devices, acts)
    member = (asked2[None, :] == jnp.arange(br_cum.shape[0], dtype=I32)[:, None]).astype(F32)
    action_value = jnp.dot(member, incoming, precision=lax.Precision.HIGHEST)
    br_policy = br_cum / jnp.sum(br_cum, axis=1, keepdims=True)
    regret_gap = jnp.max(action_value, axis=1) - jnp.sum(br_policy * action_value, axis=1)
    totals = functools.reduce(lax.psum, AXES, jnp.stack([jnp.sum(regret_gap), jnp.sum(reach)]))
    return history_value.reshape(-1), regret_gap, totals[0] / totals[1]


def solution(mesh):
    torus = Mesh(mesh.devices.reshape(4, 2, 4, 4), AXES)
    rows, flat = P(AXES, None), P(AXES)
    placed = (rows, rows, flat, P(), rows, flat, flat, P(), rows)
    return jax.shard_map(
        local, mesh=torus, in_specs=placed, out_specs=(flat, flat, P()), check_vma=False
    )
```

```python
import functools

import jax
import jax.numpy as jnp
from jax import lax
from jax.experimental import pallas as pl
from jax.experimental.pallas import tpu as pltpu
from jax.sharding import Mesh
from jax.sharding import PartitionSpec as P

AXES = ("gx_0", "gx_1", "gy_0", "gy_1")
F32, BF16, I32 = jnp.float32, jnp.bfloat16, jnp.int32
NT = (((1,), (1,)), ((), ()))


def rows_iota(rows, cols):
    return lax.broadcasted_iota(I32, (rows, cols), 0)


def lanes_iota(rows, cols):
    return lax.broadcasted_iota(I32, (rows, cols), 1)


def dot(a, b):
    return jnp.dot(a, b, preferred_element_type=F32)


def one_hot_rows(rows, index):
    return (rows_iota(rows, index.shape[1]) == index).astype(F32).astype(BF16)


def pick(table, index, base=0):
    rows, n = table.shape
    mark = rows_iota(rows, n) == index
    return jnp.sum(jnp.where(mark, table, 0.0), axis=0, keepdims=True)


BLOCK = 8


def route_kernel(set_ref, home_ref, set2_ref, home2_ref,
                 want_ref, source_ref, place_ref, place2_ref,
                 table, acc, carry):
    devices, slots = want_ref.shape
    home = home_ref[...]
    table[0:128, :] = ((home >> 9) - 256).astype(F32).T.astype(BF16)
    table[128:256, :] = ((home & 511) - 256).astype(F32).T.astype(BF16)
    acc[...] = jnp.zeros_like(acc)
    carry[...] = jnp.zeros_like(carry)
    upper = jnp.concatenate(
        [(rows_iota(128, 128) < lanes_iota(128, 128)).astype(F32), jnp.ones((128, 128), F32)], axis=1
    ).astype(BF16)

    def block(b, _):
        at = pl.ds(pl.multiple_of(b * BLOCK, BLOCK), BLOCK)
        index = set_ref[at, :]
        high, low = index >> 7, index & 127
        found = jnp.zeros((256, BLOCK * 128), F32)
        for c in range(table.shape[1] // 256):
            marks = jnp.concatenate(
                [one_hot_rows(256, high[j : j + 1, :] - 256 * c) for j in range(BLOCK)], axis=1
            )
            found += dot(table[:, 256 * c : 256 * (c + 1)], marks)
        members, values = [], []
        for j in range(BLOCK):
            lanes = slice(128 * j, 128 * (j + 1))
            mine = low[j : j + 1, :]
            top = pick(found[0:128, lanes], mine).astype(I32) + 256
            bottom = pick(found[128:256, lanes], mine).astype(I32) + 256
            row = (top << 9) + bottom
            owner, local = row >> 11, row & 2047
            member = rows_iota(128, 128) == owner
            member16 = member.astype(F32).astype(BF16)
            ahead = dot(member16, upper)
            rank = jnp.sum(
                jnp.where(member, ahead[:, :128] + carry[...], 0.0), axis=0, keepdims=True
            ).astype(I32)
            carry[...] += ahead[:, 128:]
            place_ref[pl.ds(b * BLOCK + j, 1), :] = owner * slots + rank
            mark = rows_iota(slots, 128) == rank
            lane = lanes_iota(1, 128).astype(F32)
            values.append(
                jnp.concatenate(
                    [
                        jnp.where(mark, (local >> 6).astype(F32), 0.0),
                        jnp.where(mark, (local & 63).astype(F32), 0.0),
                        jnp.where(mark, (b * BLOCK + j).astype(F32), 0.0),
                        jnp.where(mark, lane, 0.0),
                    ],
                    axis=0,
                ).astype(BF16)
            )
            members.append(member16)
        acc[...] += lax.dot_general(
            jnp.concatenate(members, axis=1),
            jnp.concatenate(values, axis=1),
            NT,
            preferred_element_type=F32,
        )
        return 0

    lax.fori_loop(0, set_ref.shape[0] // BLOCK, block, 0)
    total = acc[...]
    local = total[:, :slots] * 64.0 + total[:, slots : 2 * slots]
    source = total[:, 2 * slots : 3 * slots] * 128.0 + total[:, 3 * slots :]
    source_ref[...] = source.astype(I32)

    index2 = set2_ref[...]
    home2 = home2_ref[...]
    marks2 = one_hot_rows(home2.shape[0], index2 >> 7)
    top2 = dot((home2 >> 7).astype(F32).T.astype(BF16), marks2)
    bottom2 = dot((home2 & 127).astype(F32).T.astype(BF16), marks2)
    mine2 = index2 & 127
    row2 = pick(top2, mine2).astype(I32) * 128 + pick(bottom2, mine2).astype(I32)
    owner2, local2 = row2 >> 6, row2 & 63
    member2 = rows_iota(128, 128) == owner2
    ahead2 = dot(member2.astype(F32).astype(BF16), upper)
    rank2 = jnp.sum(jnp.where(member2, ahead2[:, :128], 0.0), axis=0, keepdims=True).astype(I32)
    place2_ref[...] = owner2 * 2 + rank2
    value2 = jnp.where(rows_iota(slots, 128) == rank2, (local2 + 1).astype(F32), 0.0).astype(BF16)
    extra = lax.dot_general(
        member2.astype(F32).astype(BF16), value2, NT, preferred_element_type=F32
    )
    want_ref[...] = (local + 2048.0 * extra).astype(I32)


def route(opp_set, opp_home, br_set, br_home, devices, slots):
    hist = opp_set.shape[0]
    return pl.pallas_call(
        route_kernel,
        out_shape=(
            jax.ShapeDtypeStruct((devices, slots), I32),
            jax.ShapeDtypeStruct((devices, slots), I32),
            jax.ShapeDtypeStruct((hist // 128, 128), I32),
            jax.ShapeDtypeStruct((1, 128), I32),
        ),
        scratch_shapes=[
            pltpu.VMEM((256, opp_home.shape[0] // 128), BF16),
            pltpu.VMEM((devices, 4 * slots), F32),
            pltpu.VMEM((devices, 128), F32),
        ],
        name="route",
    )(
        opp_set.reshape(-1, 128),
        opp_home.reshape(-1, 128),
        br_set.reshape(1, -1),
        br_home.reshape(-1, 128),
    )


def split(x):
    high = x.astype(BF16)
    return high, (x - high.astype(F32)).astype(BF16)


def find(pieces, rows, index, high_of, low_of):
    marks = jnp.concatenate(
        [one_hot_rows(rows, high_of(index[j : j + 1, :])) for j in range(BLOCK)], axis=1
    )
    found = dot(pieces, marks)
    half = found.shape[0] // 2
    both = found[:half, :] + found[half:, :]
    return [
        pick(both[:, 128 * j : 128 * (j + 1)], low_of(index[j : j + 1, :])) for j in range(BLOCK)
    ]


def look_up(pieces, rows, index_ref, out_ref, high_of, low_of, cast=lambda x: x):
    def block(b, _):
        at = pl.ds(pl.multiple_of(b * BLOCK, BLOCK), BLOCK)
        for j, row in enumerate(find(pieces, rows, index_ref[at, :], high_of, low_of)):
            out_ref[pl.ds(b * BLOCK + j, 1), :] = cast(row)
        return 0

    lax.fori_loop(0, index_ref.shape[0] // BLOCK, block, 0)


def exchange_kernel(sizes, source_ref, want_ref, place_ref, next_ref, place2_ref, reach_ref,
                    cum_ref, br_ref, child_ref,
                    value_ref, gap_ref, total_ref,
                    asked, columns, table, wide, send, recv, gathered, sums, jump,
                    outgoing, incoming, part, parts,
                    ask_out, ask_in, row_out, row_in, act_out, act_in, sum_out, sum_in):
    devices, slots, acts = send.shape
    me = [lax.axis_index(a) for a in AXES]

    def number(c):
        return ((c[0] * sizes[1] + c[1]) * sizes[2] + c[2]) * sizes[3] + c[3]

    my = number(me)

    def shift(i):
        q, s = i // 2, 2 * (i % 2)
        return q % 4 + s, (q // 32 + i) % 2, (q + q // 4) % 4 + s, (q + q // 16) % 2 + s

    def to(i):
        c = tuple((m + d) % n for m, d, n in zip(me, shift(i), sizes))
        return c, number(c)

    def back(i):
        return number(tuple((m + 2 * n - d) % n for m, d, n in zip(me, shift(i), sizes)))

    def copy(src, dst, out_sem, in_sem, device):
        return pltpu.make_async_remote_copy(
            src_ref=src, dst_ref=dst, send_sem=out_sem, recv_sem=in_sem,
            device_id=device, device_id_type=pl.DeviceIdType.MESH,
        )

    def each(body, first=1):
        lax.fori_loop(first, devices, lambda i, c: (body(i), c)[1], 0)

    barrier = pltpu.get_barrier_semaphore()
    each(lambda i: pl.semaphore_signal(
        barrier, inc=1, device_id=to(i)[0], device_id_type=pl.DeviceIdType.MESH))
    rows = table.shape[0]
    for p in range(4):
        cum = cum_ref[p * rows : (p + 1) * rows, :]
        policy = cum / jnp.sum(cum, axis=1, keepdims=True)
        table[:, 128 * p : 128 * (p + 1)] = policy.astype(BF16)
    pl.semaphore_wait(barrier, devices - 1)

    def request(i):
        device, n = to(i)
        copy(want_ref.at[n], asked.at[my], ask_out, ask_in, device).start()

    each(request)
    asked[my] = want_ref[my]
    wide[...] = child_ref[...].astype(F32)
    most = pl.ds(0, devices - 1)
    copy(want_ref.at[most], asked.at[most], ask_out, ask_in, tuple(me)).wait()
    for p in range(2):
        columns[128 * p : 128 * (p + 1), :] = asked[:, p, :].astype(F32).T.astype(I32)

    def served(n):
        column = jnp.sum(
            jnp.where(lanes_iota(slots, devices) == n, columns[...], 0), axis=1, keepdims=True
        ) & (4 * rows - 1)
        marks = (lanes_iota(slots, rows) == (column & (rows - 1))).astype(F32).astype(BF16)
        found = dot(marks, table[...])
        which = column // rows
        out = found[:, 384:]
        for p in range(3):
            out = jnp.where(which == p, found[:, 128 * p : 128 * (p + 1)], out)
        return out.astype(BF16)

    def launch(i):
        device, n = to(i)
        copy(send.at[n], recv.at[my], row_out, row_in.at[my], device).start()

    def serve(i):
        send[to(i)[1]] = served(to(i)[1])

        @pl.when(i > 1)
        def _():
            launch(i - 1)

    each(serve)
    launch(jnp.int32(devices - 1))
    recv[my] = served(my)

    places = place_ref[...]
    look_up(
        jnp.concatenate(
            [((places >> 8) * 256).astype(F32).astype(BF16), (places & 255).astype(F32).astype(BF16)],
            axis=0,
        ),
        128, next_ref, jump, lambda x: x & 127, lambda x: x >> 7, lambda x: x.astype(I32),
    )

    def consume(n):
        def some(g, _):
            for q in range(16):
                k = g * 16 + q
                gathered[pl.ds(k, 1), :] = wide[pl.ds(source_ref[n * slots + k], 1), :]
            return 0

        lax.fori_loop(0, slots // 16, some, 0)

    def finish(n):
        product = recv[n].astype(F32) * gathered[...]
        total = jnp.sum(product, axis=1, keepdims=True)
        sums[...] = jnp.where(lanes_iota(slots, devices) == n, total, sums[...])

    sums[...] = jnp.zeros_like(sums)
    consume(my)
    finish(my)

    def take(i):
        n = back(i)
        consume(n)
        copy(send.at[n], recv.at[n], row_out, row_in.at[n], tuple(me)).wait_recv()
        finish(n)

    each(take)
    pieces = jnp.concatenate(split(sums[...]), axis=0)
    look_up(pieces, 128, jump, part, lambda x: x >> 8, lambda x: x & 255)
    weighted = part[...] * reach_ref[...]
    high, low = split(weighted)
    for s in range(2):
        marks = (rows_iota(devices, 128) * 2 + s == place2_ref[...]).astype(F32).astype(BF16)
        outgoing[:, s, :] = dot(marks, high) + dot(marks, low)

    def act(i):
        device, n = to(i)
        copy(outgoing.at[n], incoming.at[my], act_out, act_in, device).start()

    each(act)
    incoming[my] = outgoing[my]
    look_up(pieces, 128, place_ref, value_ref, lambda x: x >> 8, lambda x: x & 255)
    copy(outgoing.at[most], incoming.at[most], act_out, act_in, tuple(me)).wait()
    action = jnp.zeros((br_ref.shape[0], acts), F32)
    for s in range(2):
        owned = columns[s : s + 1, :] >> 11
        member = (rows_iota(br_ref.shape[0], devices) + 1 == owned).astype(F32).astype(BF16)
        high, low = split(incoming[:, s, :])
        action += dot(member, high) + dot(member, low)
    br = br_ref[...]
    br_policy = br / jnp.sum(br, axis=1, keepdims=True)
    gap = jnp.max(action, axis=1, keepdims=True) - jnp.sum(br_policy * action, axis=1, keepdims=True)
    across = jnp.where(rows_iota(gap.shape[0], 128) == lanes_iota(gap.shape[0], 128), gap, 0.0)
    gap_row = jnp.sum(across, axis=0, keepdims=True)
    gap_ref[...] = gap_row[:, : gap_ref.shape[1]]
    lane = lanes_iota(1, 128)
    both = jnp.where(
        lane == 0,
        jnp.sum(gap_row, axis=1, keepdims=True),
        jnp.where(lane == 1, jnp.sum(reach_ref[...], axis=0, keepdims=True), 0.0),
    )
    parts[my] = both
    total_ref[...] = both

    def tell(i):
        device, n = to(i)
        copy(total_ref, parts.at[my], sum_out, sum_in, device).start()

    each(tell)
    copy(parts.at[most], parts.at[most], sum_out, sum_in, tuple(me)).wait()
    total = jnp.sum(parts[:, 0, :], axis=0, keepdims=True)
    top = jnp.sum(jnp.where(lane == 0, total, 0.0), axis=1, keepdims=True)
    bottom = jnp.sum(jnp.where(lane == 1, total, 0.0), axis=1, keepdims=True)
    total_ref[...] = jnp.broadcast_to(top / bottom, (1, 128))
    copy(send.at[most], recv.at[most], row_out, row_in.at[0], tuple(me)).wait_send()


def exchange(sizes, source, want, place, child_row, place2, reach, opp_cum, br_cum, child_value):
    devices, slots = want.shape
    hist, acts = child_value.shape
    rows = opp_cum.shape[0] // 4
    vmem, smem = pl.BlockSpec(memory_space=pltpu.VMEM), pl.BlockSpec(memory_space=pltpu.SMEM)
    dma = pltpu.SemaphoreType.DMA
    return pl.pallas_call(
        functools.partial(exchange_kernel, sizes),
        in_specs=[smem] + [vmem] * 8,
        out_specs=[vmem] * 3,
        out_shape=(
            jax.ShapeDtypeStruct((hist // 128, 128), F32),
            jax.ShapeDtypeStruct((1, br_cum.shape[0]), F32),
            jax.ShapeDtypeStruct((1, 128), F32),
        ),
        scratch_shapes=[
            pltpu.VMEM((devices, 2, 128), I32),
            pltpu.VMEM((slots, devices), I32),
            pltpu.VMEM((rows, 4 * acts), BF16),
            pltpu.VMEM((hist, acts), F32),
            pltpu.VMEM((devices, slots, acts), BF16),
            pltpu.VMEM((devices, slots, acts), BF16),
            pltpu.VMEM((slots, acts), F32),
            pltpu.VMEM((slots, devices), F32),
            pltpu.VMEM((128, 128), I32),
            pltpu.VMEM((devices, 2, acts), F32),
            pltpu.VMEM((devices, 2, acts), F32),
            pltpu.VMEM((128, 128), F32),
            pltpu.VMEM((devices, 1, 128), F32),
            dma, dma, dma, dma((devices,)), dma, dma, dma, dma,
        ],
        compiler_params=pltpu.CompilerParams(collective_id=0, has_side_effects=True),
        name="exchange",
    )(
        source.reshape(-1),
        want.reshape(devices, 2, 128),
        place,
        child_row.reshape(-1, 128),
        place2,
        reach.reshape(-1, 1),
        opp_cum,
        br_cum,
        child_value,
    )


def local(child_value, child_row, opp_set, opp_home, opp_cum, reach, br_set, br_home, br_cum):
    sizes = tuple(lax.axis_size(a) for a in AXES)
    devices = lax.axis_size(AXES)
    slots = 2 * child_value.shape[0] // devices
    want, source, place, place2 = route(opp_set, opp_home, br_set, br_home, devices, slots)
    history_value, gap, ratio = exchange(
        sizes, source, want, place, child_row, place2, reach, opp_cum, br_cum, child_value
    )
    return history_value.reshape(-1), gap.reshape(-1), ratio[0, 0]


def solution(mesh):
    torus = Mesh(mesh.devices.reshape(4, 2, 4, 4), AXES)
    rows, flat = P(AXES, None), P(AXES)
    placed = (rows, rows, flat, P(), rows, flat, flat, P(), rows)
    return jax.shard_map(
        local, mesh=torus, in_specs=placed, out_specs=(flat, flat, P()), check_vma=False
    )
```

```python
import functools

import jax
import jax.numpy as jnp
from jax import lax
from jax.experimental import pallas as pl
from jax.experimental.pallas import tpu as pltpu
from jax.sharding import Mesh
from jax.sharding import PartitionSpec as P

AXES = ("gx_0", "gx_1", "gy_0", "gy_1")
F32, BF16, I32 = jnp.float32, jnp.bfloat16, jnp.int32
NT = (((1,), (1,)), ((), ()))


def rows_iota(rows, cols):
    return lax.broadcasted_iota(I32, (rows, cols), 0)


def lanes_iota(rows, cols):
    return lax.broadcasted_iota(I32, (rows, cols), 1)


def dot(a, b):
    return jnp.dot(a, b, preferred_element_type=F32)


def one_hot_rows(rows, index):
    return (rows_iota(rows, index.shape[1]) == index).astype(F32).astype(BF16)


def pick(table, index, base=0):
    rows, n = table.shape
    mark = rows_iota(rows, n) == index
    return jnp.sum(jnp.where(mark, table, 0.0), axis=0, keepdims=True)


BLOCK = 8


def route_kernel(set_ref, home_ref, set2_ref, home2_ref,
                 want_ref, source_ref, place_ref, place2_ref,
                 table, acc, carry):
    devices, slots = want_ref.shape[0], 256
    wide = table.shape[1]
    for q in range(4):
        home = home_ref[pl.ds(q, wide, stride=4), :]
        table[128 * q : 128 * (q + 1), :] = ((home >> 9) - 256).astype(F32).T.astype(BF16)
        table[512 + 128 * q : 512 + 128 * (q + 1), :] = (
            ((home & 511) - 256).astype(F32).T.astype(BF16)
        )
    acc[...] = jnp.zeros_like(acc)
    carry[...] = jnp.zeros_like(carry)
    upper = jnp.concatenate(
        [(rows_iota(128, 128) < lanes_iota(128, 128)).astype(F32), jnp.ones((128, 128), F32)], axis=1
    ).astype(BF16)

    def block(b, _):
        at = pl.ds(pl.multiple_of(b * BLOCK, BLOCK), BLOCK)
        index = set_ref[at, :]
        high, low = index >> 9, index & 511
        marks = jnp.concatenate(
            [one_hot_rows(wide, high[j : j + 1, :]) for j in range(BLOCK)], axis=1
        )
        found = dot(table[...], marks)
        members, values = [], []
        for j in range(BLOCK):
            lanes = slice(128 * j, 128 * (j + 1))
            mine = low[j : j + 1, :]
            top = pick(found[0:512, lanes], mine).astype(I32) + 256
            bottom = pick(found[512:1024, lanes], mine).astype(I32) + 256
            row = (top << 9) + bottom
            owner, local = row >> 11, row & 2047
            member = rows_iota(128, 128) == owner
            member16 = member.astype(F32).astype(BF16)
            ahead = dot(member16, upper)
            rank = jnp.sum(
                jnp.where(member, ahead[:, :128] + carry[...], 0.0), axis=0, keepdims=True
            ).astype(I32)
            carry[...] += ahead[:, 128:]
            place_ref[pl.ds(b * BLOCK + j, 1), :] = owner * slots + rank
            mark = rows_iota(slots, 128) == rank
            code = ((b * BLOCK + j) * 128 + lanes_iota(1, 128)) * 2048 + local
            values.append(
                jnp.concatenate(
                    [
                        jnp.where(mark, piece.astype(F32), 0.0)
                        for piece in (code >> 18, ((code >> 9) & 511) - 256, (code & 511) - 256)
                    ],
                    axis=0,
                ).astype(BF16)
            )
            members.append(member16)
        acc[...] += lax.dot_general(
            jnp.concatenate(members, axis=1),
            jnp.concatenate(values, axis=1),
            NT,
            preferred_element_type=F32,
        )
        return 0

    lax.fori_loop(0, set_ref.shape[0] // BLOCK, block, 0)
    total = acc[...]
    first, second, third = (
        total[:, slots * p : slots * (p + 1)].astype(I32) for p in range(3)
    )
    code = (first << 18) + ((second + 256) << 9) + third + 256
    local, source = code & 2047, code >> 11
    for p in range(2):
        source_ref[pl.ds(p, devices, stride=2), :] = source[:, 128 * p : 128 * (p + 1)]
    index2 = set2_ref[...]
    home2 = home2_ref[...]
    marks2 = one_hot_rows(home2.shape[0], index2 >> 7)
    top2 = dot((home2 >> 7).astype(F32).T.astype(BF16), marks2)
    bottom2 = dot((home2 & 127).astype(F32).T.astype(BF16), marks2)
    mine2 = index2 & 127
    row2 = pick(top2, mine2).astype(I32) * 128 + pick(bottom2, mine2).astype(I32)
    owner2, local2 = row2 >> 6, row2 & 63
    member2 = rows_iota(128, 128) == owner2
    ahead2 = dot(member2.astype(F32).astype(BF16), upper)
    rank2 = jnp.sum(jnp.where(member2, ahead2[:, :128], 0.0), axis=0, keepdims=True).astype(I32)
    place2_ref[...] = owner2 * 2 + rank2
    value2 = jnp.where(rows_iota(slots, 128) == rank2, (local2 + 1).astype(F32), 0.0).astype(BF16)
    extra = lax.dot_general(
        member2.astype(F32).astype(BF16), value2, NT, preferred_element_type=F32
    )
    wanted = local + (extra.astype(I32) << 11)
    for p in range(2):
        want_ref[:, p, :] = wanted[:, 128 * p : 128 * (p + 1)]


def route(opp_set, opp_home, br_set, br_home, devices, slots):
    hist = opp_set.shape[0]
    return pl.pallas_call(
        route_kernel,
        out_shape=(
            jax.ShapeDtypeStruct((devices, 2, slots // 2), I32),
            jax.ShapeDtypeStruct((2 * devices, slots // 2), I32),
            jax.ShapeDtypeStruct((hist // 128, 128), I32),
            jax.ShapeDtypeStruct((1, 128), I32),
        ),
        scratch_shapes=[
            pltpu.VMEM((1024, opp_home.shape[0] // 512), BF16),
            pltpu.VMEM((devices, 3 * slots), F32),
            pltpu.VMEM((devices, 128), F32),
        ],
        name="route",
    )(
        opp_set.reshape(-1, 128),
        opp_home.reshape(-1, 128),
        br_set.reshape(1, -1),
        br_home.reshape(-1, 128),
    )


def split(x):
    high = x.astype(BF16)
    return high, (x - high.astype(F32)).astype(BF16)


def find(pieces, rows, index, high_of, low_of):
    marks = jnp.concatenate(
        [one_hot_rows(rows, high_of(index[j : j + 1, :])) for j in range(BLOCK)], axis=1
    )
    found = dot(pieces, marks)
    half = found.shape[0] // 2
    both = found[:half, :] + found[half:, :]
    return [
        pick(both[:, 128 * j : 128 * (j + 1)], low_of(index[j : j + 1, :])) for j in range(BLOCK)
    ]


def look_up(pieces, rows, index_ref, out_ref, high_of, low_of, cast=lambda x: x):
    def block(b, _):
        at = pl.ds(pl.multiple_of(b * BLOCK, BLOCK), BLOCK)
        for j, row in enumerate(find(pieces, rows, index_ref[at, :], high_of, low_of)):
            out_ref[pl.ds(b * BLOCK + j, 1), :] = cast(row)
        return 0

    lax.fori_loop(0, index_ref.shape[0] // BLOCK, block, 0)


def exchange_kernel(sizes, source_ref, want_ref, place_ref, next_ref, place2_ref, reach_ref,
                    cum_ref, br_ref, child_ref,
                    value_ref, gap_ref, total_ref,
                    asked, columns, table, wide, send, recv, gathered, sums, jump,
                    outgoing, incoming, part, parts,
                    ask_out, ask_in, row_out, row_in, act_out, act_in, sum_out, sum_in):
    devices, slots, acts = send.shape
    me = [lax.axis_index(a) for a in AXES]

    def number(c):
        return ((c[0] * sizes[1] + c[1]) * sizes[2] + c[2]) * sizes[3] + c[3]

    my = number(me)

    def rem(x, n):
        return lax.rem(x, jnp.int32(n))

    def div(x, n):
        return lax.div(x, jnp.int32(n))

    def shift(i):
        q, s = div(i, 2), 2 * rem(i, 2)
        return (
            rem(q, 4) + s,
            rem(div(q, 32) + i, 2),
            rem(q + div(q, 4), 4) + s,
            rem(q + div(q, 16), 2) + s,
        )

    def to(i):
        c = tuple(rem(m + d, n) for m, d, n in zip(me, shift(i), sizes))
        return c, number(c)

    def back(i):
        return number(tuple(rem(m + 2 * n - d, n) for m, d, n in zip(me, shift(i), sizes)))

    def copy(src, dst, out_sem, in_sem, device):
        return pltpu.make_async_remote_copy(
            src_ref=src, dst_ref=dst, send_sem=out_sem, recv_sem=in_sem,
            device_id=device, device_id_type=pl.DeviceIdType.MESH,
        )

    def each(body, first=1):
        lax.fori_loop(first, devices, lambda i, c: (body(i), c)[1], 0)

    barrier = pltpu.get_barrier_semaphore()
    each(lambda i: pl.semaphore_signal(
        barrier, inc=1, device_id=to(i)[0], device_id_type=pl.DeviceIdType.MESH))
    rows = table.shape[0]
    for p in range(4):
        cum = cum_ref[p * rows : (p + 1) * rows, :]
        policy = cum / jnp.sum(cum, axis=1, keepdims=True)
        table[:, 128 * p : 128 * (p + 1)] = policy.astype(BF16)
    pl.semaphore_wait(barrier, devices - 1)

    def request(i):
        device, n = to(i)
        copy(want_ref.at[n], asked.at[my], ask_out, ask_in, device).start()

    each(request)
    asked[my] = want_ref[my]
    wide[...] = child_ref[...].astype(F32)
    places = place_ref[...]
    look_up(
        jnp.concatenate(
            [((places >> 8) * 256).astype(F32).astype(BF16), (places & 255).astype(F32).astype(BF16)],
            axis=0,
        ),
        128, next_ref, jump, lambda x: x & 127, lambda x: x >> 7, lambda x: x.astype(I32),
    )
    most = pl.ds(0, devices - 1)
    copy(want_ref.at[most], asked.at[most], ask_out, ask_in, tuple(me)).wait()
    for p in range(2):
        columns[128 * p : 128 * (p + 1), :] = asked[:, p, :].astype(F32).T.astype(I32)

    def served(n):
        column = jnp.sum(
            jnp.where(lanes_iota(slots, devices) == n, columns[...], 0), axis=1, keepdims=True
        ) & (4 * rows - 1)
        marks = (lanes_iota(slots, rows) == (column & (rows - 1))).astype(F32).astype(BF16)
        found = dot(marks, table[...])
        which = column // rows
        out = found[:, 384:]
        for p in range(3):
            out = jnp.where(which == p, found[:, 128 * p : 128 * (p + 1)], out)
        return out.astype(BF16)

    def launch(i):
        device, n = to(i)
        copy(send.at[n], recv.at[my], row_out, row_in.at[my], device).start()

    def serve(i):
        send[to(i)[1]] = served(to(i)[1])

        @pl.when(i > 1)
        def _():
            launch(i - 1)

    each(serve)
    launch(jnp.int32(devices - 1))
    recv[my] = served(my)

    def consume(n):
        def some(g, _):
            row, start = 2 * n + g, pl.multiple_of(g * 128, 128)
            for q in range(128):
                gathered[pl.ds(start + q, 1), :] = wide[pl.ds(source_ref[row, q], 1), :]
            return 0

        lax.fori_loop(0, 2, some, 0)

    def finish(n):
        product = recv[n].astype(F32) * gathered[...]
        total = jnp.sum(product, axis=1, keepdims=True)
        sums[...] = jnp.where(lanes_iota(slots, devices) == n, total, sums[...])

    sums[...] = jnp.zeros_like(sums)
    consume(my)
    finish(my)

    def take(i):
        n = back(i)
        consume(n)
        copy(send.at[n], recv.at[n], row_out, row_in.at[n], tuple(me)).wait_recv()
        finish(n)

    each(take)
    pieces = jnp.concatenate(split(sums[...]), axis=0)
    look_up(pieces, 128, jump, part, lambda x: x >> 8, lambda x: x & 255)
    reach = jnp.sum(
        jnp.where(rows_iota(128, 128) == lanes_iota(128, 128), reach_ref[...], 0.0),
        axis=1, keepdims=True,
    )
    weighted = part[...] * reach
    high, low = split(weighted)
    for s in range(2):
        marks = (rows_iota(devices, 128) * 2 + s == place2_ref[...]).astype(F32).astype(BF16)
        outgoing[:, s, :] = dot(marks, high) + dot(marks, low)

    def act(i):
        device, n = to(i)
        copy(outgoing.at[n], incoming.at[my], act_out, act_in, device).start()

    each(act)
    incoming[my] = outgoing[my]
    look_up(pieces, 128, place_ref, value_ref, lambda x: x >> 8, lambda x: x & 255)
    copy(outgoing.at[most], incoming.at[most], act_out, act_in, tuple(me)).wait()
    action = jnp.zeros((br_ref.shape[0], acts), F32)
    for s in range(2):
        owned = columns[s : s + 1, :] >> 11
        member = (rows_iota(br_ref.shape[0], devices) + 1 == owned).astype(F32).astype(BF16)
        high, low = split(incoming[:, s, :])
        action += dot(member, high) + dot(member, low)
    br = br_ref[...]
    br_policy = br / jnp.sum(br, axis=1, keepdims=True)
    gap = jnp.max(action, axis=1, keepdims=True) - jnp.sum(br_policy * action, axis=1, keepdims=True)
    across = jnp.where(rows_iota(gap.shape[0], 128) == lanes_iota(gap.shape[0], 128), gap, 0.0)
    gap_row = jnp.sum(across, axis=0, keepdims=True)
    gap_ref[...] = gap_row[:, : gap_ref.shape[1]]
    lane = lanes_iota(1, 128)
    both = jnp.where(
        lane == 0,
        jnp.sum(gap_row, axis=1, keepdims=True),
        jnp.where(lane == 1, jnp.sum(reach_ref[...], axis=1, keepdims=True), 0.0),
    )
    parts[my] = both
    total_ref[...] = both

    def tell(i):
        device, n = to(i)
        copy(total_ref, parts.at[my], sum_out, sum_in, device).start()

    each(tell)
    copy(parts.at[most], parts.at[most], sum_out, sum_in, tuple(me)).wait()
    total = jnp.sum(parts[:, 0, :], axis=0, keepdims=True)
    top = jnp.sum(jnp.where(lane == 0, total, 0.0), axis=1, keepdims=True)
    bottom = jnp.sum(jnp.where(lane == 1, total, 0.0), axis=1, keepdims=True)
    total_ref[...] = jnp.broadcast_to(top / bottom, (1, 128))
    copy(send.at[most], recv.at[most], row_out, row_in.at[0], tuple(me)).wait_send()


def exchange(sizes, source, want, place, child_row, place2, reach, opp_cum, br_cum, child_value):
    devices, slots = want.shape[0], want.shape[1] * want.shape[2]
    hist, acts = child_value.shape
    rows = opp_cum.shape[0] // 4
    vmem, smem = pl.BlockSpec(memory_space=pltpu.VMEM), pl.BlockSpec(memory_space=pltpu.SMEM)
    dma = pltpu.SemaphoreType.DMA
    return pl.pallas_call(
        functools.partial(exchange_kernel, sizes),
        in_specs=[smem] + [vmem] * 8,
        out_specs=[vmem] * 3,
        out_shape=(
            jax.ShapeDtypeStruct((hist // 128, 128), F32),
            jax.ShapeDtypeStruct((1, br_cum.shape[0]), F32),
            jax.ShapeDtypeStruct((1, 128), F32),
        ),
        scratch_shapes=[
            pltpu.VMEM((devices, 2, 128), I32),
            pltpu.VMEM((slots, devices), I32),
            pltpu.VMEM((rows, 4 * acts), BF16),
            pltpu.VMEM((hist, acts), F32),
            pltpu.VMEM((devices, slots, acts), BF16),
            pltpu.VMEM((devices, slots, acts), BF16),
            pltpu.VMEM((slots, acts), F32),
            pltpu.VMEM((slots, devices), F32),
            pltpu.VMEM((128, 128), I32),
            pltpu.VMEM((devices, 2, acts), F32),
            pltpu.VMEM((devices, 2, acts), F32),
            pltpu.VMEM((128, 128), F32),
            pltpu.VMEM((devices, 1, 128), F32),
            dma, dma, dma, dma((devices,)), dma, dma, dma, dma,
        ],
        compiler_params=pltpu.CompilerParams(collective_id=0, has_side_effects=True),
        name="exchange",
    )(
        source,
        want,
        place,
        child_row.reshape(-1, 128),
        place2,
        reach.reshape(1, -1),
        opp_cum,
        br_cum,
        child_value,
    )


def local(child_value, child_row, opp_set, opp_home, opp_cum, reach, br_set, br_home, br_cum):
    sizes = tuple(lax.axis_size(a) for a in AXES)
    devices = lax.axis_size(AXES)
    slots = 2 * child_value.shape[0] // devices
    want, source, place, place2 = route(opp_set, opp_home, br_set, br_home, devices, slots)
    history_value, gap, ratio = exchange(
        sizes, source, want, place, child_row, place2, reach, opp_cum, br_cum, child_value
    )
    return history_value.reshape(-1), gap.reshape(-1), ratio[0, 0]


def solution(mesh):
    torus = Mesh(mesh.devices.reshape(4, 2, 4, 4), AXES)
    rows, flat = P(AXES, None), P(AXES)
    placed = (rows, rows, flat, P(), rows, flat, flat, P(), rows)
    return jax.shard_map(
        local, mesh=torus, in_specs=placed, out_specs=(flat, flat, P()), check_vma=False
    )
```

```python
import functools

import jax
import jax.numpy as jnp
from jax import lax
from jax.experimental import pallas as pl
from jax.experimental.pallas import tpu as pltpu
from jax.sharding import Mesh
from jax.sharding import PartitionSpec as P

AXES = ("gx_0", "gx_1", "gy_0", "gy_1")
F32, BF16, I32 = jnp.float32, jnp.bfloat16, jnp.int32
NT = (((1,), (1,)), ((), ()))


def rows_iota(rows, cols):
    return lax.broadcasted_iota(I32, (rows, cols), 0)


def lanes_iota(rows, cols):
    return lax.broadcasted_iota(I32, (rows, cols), 1)


def dot(a, b):
    return jnp.dot(a, b, preferred_element_type=F32)


def one_hot_rows(rows, index):
    return (rows_iota(rows, index.shape[1]) == index).astype(F32).astype(BF16)


def pick(table, index, base=0):
    rows, n = table.shape
    mark = rows_iota(rows, n) == index
    return jnp.sum(jnp.where(mark, table, 0.0), axis=0, keepdims=True)


BLOCK = 8


def route_kernel(set_ref, home_ref, set2_ref, home2_ref,
                 want_ref, source_ref, place_ref, place2_ref,
                 table, acc, carry):
    devices, slots = want_ref.shape[0], 256
    wide = table.shape[1]
    for q in range(4):
        home = home_ref[pl.ds(q, wide, stride=4), :]
        table[128 * q : 128 * (q + 1), :] = ((home >> 9) - 256).astype(F32).T.astype(BF16)
        table[512 + 128 * q : 512 + 128 * (q + 1), :] = (
            ((home & 511) - 256).astype(F32).T.astype(BF16)
        )
    acc[...] = jnp.zeros_like(acc)
    carry[...] = jnp.zeros_like(carry)
    upper = jnp.concatenate(
        [(rows_iota(128, 128) < lanes_iota(128, 128)).astype(F32), jnp.ones((128, 128), F32)], axis=1
    ).astype(BF16)

    def block(b, _):
        at = pl.ds(pl.multiple_of(b * BLOCK, BLOCK), BLOCK)
        index = set_ref[at, :]
        high, low = index >> 9, index & 511
        each = BLOCK // 2
        marks = [
            jnp.concatenate(
                [one_hot_rows(wide, high[j : j + 1, :]) for j in range(h * each, (h + 1) * each)],
                axis=1,
            )
            for h in range(2)
        ]
        halves = [dot(table[...], m) for m in marks]
        members, values = [], []
        for j in range(BLOCK):
            found, at_lane = halves[j // each], j % each
            lanes = slice(128 * at_lane, 128 * (at_lane + 1))
            mine = low[j : j + 1, :]
            top = pick(found[0:512, lanes], mine).astype(I32) + 256
            bottom = pick(found[512:1024, lanes], mine).astype(I32) + 256
            row = (top << 9) + bottom
            owner, local = row >> 11, row & 2047
            member = rows_iota(128, 128) == owner
            member16 = member.astype(F32).astype(BF16)
            ahead = dot(member16, upper)
            rank = jnp.sum(
                jnp.where(member, ahead[:, :128] + carry[...], 0.0), axis=0, keepdims=True
            ).astype(I32)
            carry[...] += ahead[:, 128:]
            place_ref[pl.ds(b * BLOCK + j, 1), :] = owner * slots + rank
            mark = rows_iota(slots, 128) == rank
            code = ((b * BLOCK + j) * 128 + lanes_iota(1, 128)) * 2048 + local
            values.append(
                jnp.concatenate(
                    [
                        jnp.where(mark, piece.astype(F32), 0.0)
                        for piece in (code >> 18, ((code >> 9) & 511) - 256, (code & 511) - 256)
                    ],
                    axis=0,
                ).astype(BF16)
            )
            members.append(member16)
        acc[...] += lax.dot_general(
            jnp.concatenate(members, axis=1),
            jnp.concatenate(values, axis=1),
            NT,
            preferred_element_type=F32,
        )
        return 0

    lax.fori_loop(0, set_ref.shape[0] // BLOCK, block, 0)
    total = acc[...]
    first, second, third = (
        total[:, slots * p : slots * (p + 1)].astype(I32) for p in range(3)
    )
    code = (first << 18) + ((second + 256) << 9) + third + 256
    local, source = code & 2047, code >> 11
    for p in range(2):
        source_ref[pl.ds(p, devices, stride=2), :] = source[:, 128 * p : 128 * (p + 1)]
    index2 = set2_ref[...]
    home2 = home2_ref[...]
    marks2 = one_hot_rows(home2.shape[0], index2 >> 7)
    top2 = dot((home2 >> 7).astype(F32).T.astype(BF16), marks2)
    bottom2 = dot((home2 & 127).astype(F32).T.astype(BF16), marks2)
    mine2 = index2 & 127
    row2 = pick(top2, mine2).astype(I32) * 128 + pick(bottom2, mine2).astype(I32)
    owner2, local2 = row2 >> 6, row2 & 63
    member2 = rows_iota(128, 128) == owner2
    ahead2 = dot(member2.astype(F32).astype(BF16), upper)
    rank2 = jnp.sum(jnp.where(member2, ahead2[:, :128], 0.0), axis=0, keepdims=True).astype(I32)
    place2_ref[...] = owner2 * 2 + rank2
    value2 = jnp.where(rows_iota(slots, 128) == rank2, (local2 + 1).astype(F32), 0.0).astype(BF16)
    extra = lax.dot_general(
        member2.astype(F32).astype(BF16), value2, NT, preferred_element_type=F32
    )
    wanted = local + (extra.astype(I32) << 11)
    for p in range(2):
        want_ref[:, p, :] = wanted[:, 128 * p : 128 * (p + 1)]


def route(opp_set, opp_home, br_set, br_home, devices, slots):
    hist = opp_set.shape[0]
    return pl.pallas_call(
        route_kernel,
        out_shape=(
            jax.ShapeDtypeStruct((devices, 2, slots // 2), I32),
            jax.ShapeDtypeStruct((2 * devices, slots // 2), I32),
            jax.ShapeDtypeStruct((hist // 128, 128), I32),
            jax.ShapeDtypeStruct((1, 128), I32),
        ),
        scratch_shapes=[
            pltpu.VMEM((1024, opp_home.shape[0] // 512), BF16),
            pltpu.VMEM((devices, 3 * slots), F32),
            pltpu.VMEM((devices, 128), F32),
        ],
        name="route",
    )(
        opp_set.reshape(-1, 128),
        opp_home.reshape(-1, 128),
        br_set.reshape(1, -1),
        br_home.reshape(-1, 128),
    )


def split(x):
    high = x.astype(BF16)
    return high, (x - high.astype(F32)).astype(BF16)


def find(pieces, rows, index, high_of, low_of):
    marks = jnp.concatenate(
        [one_hot_rows(rows, high_of(index[j : j + 1, :])) for j in range(BLOCK)], axis=1
    )
    found = dot(pieces, marks)
    half = found.shape[0] // 2
    both = found[:half, :] + found[half:, :]
    return [
        pick(both[:, 128 * j : 128 * (j + 1)], low_of(index[j : j + 1, :])) for j in range(BLOCK)
    ]


def look_up(pieces, rows, index_ref, out_ref, high_of, low_of, cast=lambda x: x):
    def block(b, _):
        at = pl.ds(pl.multiple_of(b * BLOCK, BLOCK), BLOCK)
        for j, row in enumerate(find(pieces, rows, index_ref[at, :], high_of, low_of)):
            out_ref[pl.ds(b * BLOCK + j, 1), :] = cast(row)
        return 0

    lax.fori_loop(0, index_ref.shape[0] // BLOCK, block, 0)


def exchange_kernel(sizes, source_ref, want_ref, place_ref, next_ref, place2_ref, reach_ref,
                    cum_ref, br_ref, child_ref,
                    value_ref, gap_ref, total_ref,
                    asked, columns, table, wide, send, recv, gathered, sums, jump,
                    outgoing, incoming, part, parts_one, parts_two, middle_ref, ask_mid, act_mid,
                    ask_sems, row_out, row_in, act_sems, sum_sems):
    devices, slots, acts = send.shape
    me = [lax.axis_index(a) for a in AXES]

    def number(c):
        return ((c[0] * sizes[1] + c[1]) * sizes[2] + c[2]) * sizes[3] + c[3]

    my = number(me)

    def rem(x, n):
        return lax.rem(x, jnp.int32(n))

    def div(x, n):
        return lax.div(x, jnp.int32(n))

    def shift(i):
        q, s = div(i, 2), 2 * rem(i, 2)
        return (
            rem(q, 4) + s,
            rem(div(q, 32) + i, 2),
            rem(q + div(q, 4), 4) + s,
            rem(q + div(q, 16), 2) + s,
        )

    def to(i):
        c = tuple(rem(m + d, n) for m, d, n in zip(me, shift(i), sizes))
        return c, number(c)

    def back(i):
        return number(tuple(rem(m + 2 * n - d, n) for m, d, n in zip(me, shift(i), sizes)))

    def copy(src, dst, out_sem, in_sem, device):
        return pltpu.make_async_remote_copy(
            src_ref=src, dst_ref=dst, send_sem=out_sem, recv_sem=in_sem,
            device_id=device, device_id_type=pl.DeviceIdType.MESH,
        )

    def each(body, first=1):
        lax.fori_loop(first, devices, lambda i, c: (body(i), c)[1], 0)

    barrier = pltpu.get_barrier_semaphore()
    each(lambda i: pl.semaphore_signal(
        barrier, inc=1, device_id=to(i)[0], device_id_type=pl.DeviceIdType.MESH))
    rows = table.shape[0]
    for p in range(4):
        cum = cum_ref[p * rows : (p + 1) * rows, :]
        policy = cum / jnp.sum(cum, axis=1, keepdims=True)
        table[:, 128 * p : 128 * (p + 1)] = policy.astype(BF16)
    pl.semaphore_wait(barrier, devices - 1)

    first, second = me[0] * sizes[1] + me[1], me[2] * sizes[3] + me[3]
    near, far = sizes[0] * sizes[1], sizes[2] * sizes[3]

    def along_first(t):
        c = rem(me[0] + div(t, sizes[1]), sizes[0]), rem(me[1] + rem(t, sizes[1]), sizes[1])
        return (*c, me[2], me[3]), c[0] * sizes[1] + c[1]

    def along_second(t):
        c = rem(me[2] + div(t, sizes[3]), sizes[2]), rem(me[3] + rem(t, sizes[3]), sizes[3])
        return (me[0], me[1], *c), c[0] * sizes[3] + c[1]

    def over(count, body):
        lax.fori_loop(1, count, lambda t, c: (body(t), c)[1], 0)

    def stage_one(source, middle, sems):
        def go(t):
            device, n = along_first(t)
            copy(source.at[n], middle.at[first], sems.at[0], sems.at[1], device).start()

        over(near, go)
        middle[first] = source[first]

    def stage_two(middle, target, sems):
        some = pl.ds(0, near - 1)
        copy(middle.at[some], middle.at[some], sems.at[0], sems.at[1], tuple(me)).wait()

        def go(t):
            device, n = along_second(t)
            copy(middle.at[:, n], target.at[:, second], sems.at[2], sems.at[3], device).start()

        over(far, go)
        target[:, second] = middle[:, second]

    def stage_end(middle, target, sems):
        some = pl.ds(0, far - 1)
        copy(middle.at[:, some], target.at[:, some], sems.at[2], sems.at[3], tuple(me)).wait()

    most = pl.ds(0, devices - 1)
    stage_one(want_ref, ask_mid, ask_sems)
    wide[...] = child_ref[...].astype(F32)
    stage_two(ask_mid, asked, ask_sems)
    places = place_ref[...]
    look_up(
        jnp.concatenate(
            [((places >> 8) * 256).astype(F32).astype(BF16), (places & 255).astype(F32).astype(BF16)],
            axis=0,
        ),
        128, next_ref, jump, lambda x: x & 127, lambda x: x >> 7, lambda x: x.astype(I32),
    )
    most = pl.ds(0, devices - 1)
    stage_end(ask_mid, asked, ask_sems)
    for p in range(2):
        rowwise = asked[:, :, p, :].reshape(devices, 128)
        columns[128 * p : 128 * (p + 1), :] = rowwise.astype(F32).T.astype(I32)

    def served(n):
        column = jnp.sum(
            jnp.where(lanes_iota(slots, devices) == n, columns[...], 0), axis=1, keepdims=True
        ) & (4 * rows - 1)
        marks = (lanes_iota(slots, rows) == (column & (rows - 1))).astype(F32).astype(BF16)
        found = dot(marks, table[...])
        which = column // rows
        out = found[:, 384:]
        for p in range(3):
            out = jnp.where(which == p, found[:, 128 * p : 128 * (p + 1)], out)
        return out.astype(BF16)

    def launch(i):
        device, n = to(i)
        copy(send.at[n], recv.at[my], row_out, row_in.at[my], device).start()

    def serve(i):
        send[to(i)[1]] = served(to(i)[1])

        @pl.when(i > 1)
        def _():
            launch(i - 1)

    each(serve)
    launch(jnp.int32(devices - 1))
    recv[my] = served(my)

    def consume(n):
        def some(g, _):
            row, start = 2 * n + g, pl.multiple_of(g * 128, 128)
            for q in range(128):
                gathered[pl.ds(start + q, 1), :] = wide[pl.ds(source_ref[row, q], 1), :]
            return 0

        lax.fori_loop(0, 2, some, 0)

    def finish(n):
        product = recv[n].astype(F32) * gathered[...]
        total = jnp.sum(product, axis=1, keepdims=True)
        sums[...] = jnp.where(lanes_iota(slots, devices) == n, total, sums[...])

    sums[...] = jnp.zeros_like(sums)
    consume(my)
    finish(my)

    def take(i):
        n = back(i)
        consume(n)
        copy(send.at[n], recv.at[n], row_out, row_in.at[n], tuple(me)).wait_recv()
        finish(n)

    each(take)
    pieces = jnp.concatenate(split(sums[...]), axis=0)
    look_up(pieces, 128, jump, part, lambda x: x >> 8, lambda x: x & 255)
    reach = jnp.sum(
        jnp.where(rows_iota(128, 128) == lanes_iota(128, 128), reach_ref[...], 0.0),
        axis=1, keepdims=True,
    )
    weighted = part[...] * reach
    high, low = split(weighted)
    for s in range(2):
        marks = (rows_iota(devices, 128) * 2 + s == place2_ref[...]).astype(F32).astype(BF16)
        outgoing[:, :, s, :] = (dot(marks, high) + dot(marks, low)).reshape(near, far, acts)

    stage_one(outgoing, act_mid, act_sems)
    stage_two(act_mid, incoming, act_sems)
    look_up(pieces, 128, place_ref, value_ref, lambda x: x >> 8, lambda x: x & 255)
    stage_end(act_mid, incoming, act_sems)
    action = jnp.zeros((br_ref.shape[0], acts), F32)
    for s in range(2):
        owned = columns[s : s + 1, :] >> 11
        member = (rows_iota(br_ref.shape[0], devices) + 1 == owned).astype(F32).astype(BF16)
        high, low = split(incoming[:, :, s, :].reshape(devices, acts))
        action += dot(member, high) + dot(member, low)
    br = br_ref[...]
    br_policy = br / jnp.sum(br, axis=1, keepdims=True)
    gap = jnp.max(action, axis=1, keepdims=True) - jnp.sum(br_policy * action, axis=1, keepdims=True)
    across = jnp.where(rows_iota(gap.shape[0], 128) == lanes_iota(gap.shape[0], 128), gap, 0.0)
    gap_row = jnp.sum(across, axis=0, keepdims=True)
    gap_ref[...] = gap_row[:, : gap_ref.shape[1]]
    lane = lanes_iota(1, 128)
    both = jnp.where(
        lane == 0,
        jnp.sum(gap_row, axis=1, keepdims=True),
        jnp.where(lane == 1, jnp.sum(reach_ref[...], axis=1, keepdims=True), 0.0),
    )
    parts_one[first] = both
    total_ref[...] = both

    def tell_first(t):
        copy(total_ref, parts_one.at[first], sum_sems.at[0], sum_sems.at[1], along_first(t)[0]).start()

    over(near, tell_first)
    some = pl.ds(0, near - 1)
    copy(parts_one.at[some], parts_one.at[some], sum_sems.at[0], sum_sems.at[1], tuple(me)).wait()
    middle = jnp.sum(parts_one[:, 0, :], axis=0, keepdims=True)
    parts_two[second] = middle
    middle_ref[...] = middle

    def tell_second(t):
        copy(middle_ref, parts_two.at[second], sum_sems.at[2], sum_sems.at[3], along_second(t)[0]).start()

    over(far, tell_second)
    some = pl.ds(0, far - 1)
    copy(parts_two.at[some], parts_two.at[some], sum_sems.at[2], sum_sems.at[3], tuple(me)).wait()
    total = jnp.sum(parts_two[:, 0, :], axis=0, keepdims=True)
    top = jnp.sum(jnp.where(lane == 0, total, 0.0), axis=1, keepdims=True)
    bottom = jnp.sum(jnp.where(lane == 1, total, 0.0), axis=1, keepdims=True)
    total_ref[...] = jnp.broadcast_to(top / bottom, (1, 128))
    copy(send.at[most], recv.at[most], row_out, row_in.at[0], tuple(me)).wait_send()


def exchange(sizes, source, want, place, child_row, place2, reach, opp_cum, br_cum, child_value):
    devices, slots = want.shape[0], want.shape[1] * want.shape[2]
    hist, acts = child_value.shape
    rows = opp_cum.shape[0] // 4
    near, far = sizes[0] * sizes[1], sizes[2] * sizes[3]
    vmem, smem = pl.BlockSpec(memory_space=pltpu.VMEM), pl.BlockSpec(memory_space=pltpu.SMEM)
    dma = pltpu.SemaphoreType.DMA
    return pl.pallas_call(
        functools.partial(exchange_kernel, sizes),
        in_specs=[smem] + [vmem] * 8,
        out_specs=[vmem] * 3,
        out_shape=(
            jax.ShapeDtypeStruct((hist // 128, 128), F32),
            jax.ShapeDtypeStruct((1, br_cum.shape[0]), F32),
            jax.ShapeDtypeStruct((1, 128), F32),
        ),
        scratch_shapes=[
            pltpu.VMEM((near, far, 2, 128), I32),
            pltpu.VMEM((slots, devices), I32),
            pltpu.VMEM((rows, 4 * acts), BF16),
            pltpu.VMEM((hist, acts), F32),
            pltpu.VMEM((devices, slots, acts), BF16),
            pltpu.VMEM((devices, slots, acts), BF16),
            pltpu.VMEM((slots, acts), F32),
            pltpu.VMEM((slots, devices), F32),
            pltpu.VMEM((128, 128), I32),
            pltpu.VMEM((near, far, 2, acts), F32),
            pltpu.VMEM((near, far, 2, acts), F32),
            pltpu.VMEM((128, 128), F32),
            pltpu.VMEM((near, 1, 128), F32),
            pltpu.VMEM((far, 1, 128), F32),
            pltpu.VMEM((1, 128), F32),
            pltpu.VMEM((near, far, 2, 128), I32),
            pltpu.VMEM((near, far, 2, acts), F32),
            dma((4,)), dma, dma((devices,)), dma((4,)), dma((4,)),
        ],
        compiler_params=pltpu.CompilerParams(collective_id=0, has_side_effects=True),
        name="exchange",
    )(
        source,
        want.reshape(near, far, 2, 128),
        place,
        child_row.reshape(-1, 128),
        place2,
        reach.reshape(1, -1),
        opp_cum,
        br_cum,
        child_value,
    )


def local(child_value, child_row, opp_set, opp_home, opp_cum, reach, br_set, br_home, br_cum):
    sizes = tuple(lax.axis_size(a) for a in AXES)
    devices = lax.axis_size(AXES)
    slots = 2 * child_value.shape[0] // devices
    want, source, place, place2 = route(opp_set, opp_home, br_set, br_home, devices, slots)
    history_value, gap, ratio = exchange(
        sizes, source, want, place, child_row, place2, reach, opp_cum, br_cum, child_value
    )
    return history_value.reshape(-1), gap.reshape(-1), ratio[0, 0]


def solution(mesh):
    torus = Mesh(mesh.devices.reshape(4, 2, 4, 4), AXES)
    rows, flat = P(AXES, None), P(AXES)
    placed = (rows, rows, flat, P(), rows, flat, flat, P(), rows)
    return jax.shard_map(
        local, mesh=torus, in_specs=placed, out_specs=(flat, flat, P()), check_vma=False
    )
```

```python
import functools

import jax
import jax.numpy as jnp
from jax import lax
from jax.experimental import pallas as pl
from jax.experimental.pallas import tpu as pltpu
from jax.sharding import Mesh
from jax.sharding import PartitionSpec as P

AXES = ("gx_0", "gx_1", "gy_0", "gy_1")
F32, BF16, I32 = jnp.float32, jnp.bfloat16, jnp.int32
NT = (((1,), (1,)), ((), ()))


def rows_iota(rows, cols):
    return lax.broadcasted_iota(I32, (rows, cols), 0)


def lanes_iota(rows, cols):
    return lax.broadcasted_iota(I32, (rows, cols), 1)


def dot(a, b):
    return jnp.dot(a, b, preferred_element_type=F32)


def one_hot_rows(rows, index):
    return (rows_iota(rows, index.shape[1]) == index).astype(F32).astype(BF16)


def pick(table, index, base=0):
    rows, n = table.shape
    mark = rows_iota(rows, n) == index
    return jnp.sum(jnp.where(mark, table, 0.0), axis=0, keepdims=True)


BLOCK = 8


def route_kernel(set_ref, home_ref, set2_ref, home2_ref,
                 want_ref, source_ref, place_ref, place2_ref,
                 table, acc, carry):
    devices, slots = want_ref.shape[0], 256
    wide = table.shape[1] // 2
    for q in range(4):
        home = home_ref[pl.ds(q, wide, stride=4), :]
        lanes = slice(128 * q, 128 * (q + 1))
        table[lanes, :wide] = (((home >> 9) - 256) * 512).astype(F32).T.astype(BF16)
        table[lanes, wide:] = ((home & 511) - 256).astype(F32).T.astype(BF16)
    acc[...] = jnp.zeros_like(acc)
    carry[...] = jnp.zeros_like(carry)
    upper = jnp.concatenate(
        [(rows_iota(128, 128) < lanes_iota(128, 128)).astype(F32), jnp.ones((128, 128), F32)], axis=1
    ).astype(BF16)

    def block(b, _):
        at = pl.ds(pl.multiple_of(b * BLOCK, BLOCK), BLOCK)
        index = set_ref[at, :]
        high, low = index >> 9, index & 511
        each = BLOCK // 2
        marks = [
            jnp.concatenate(
                [one_hot_rows(wide, high[j : j + 1, :]) for j in range(h * each, (h + 1) * each)],
                axis=1,
            )
            for h in range(2)
        ]
        halves = [dot(table[...], jnp.concatenate([m, m], axis=0)) for m in marks]
        members, values = [], []
        for j in range(BLOCK):
            found, at_lane = halves[j // each], j % each
            lanes = slice(128 * at_lane, 128 * (at_lane + 1))
            mine = low[j : j + 1, :]
            row = pick(found[:, lanes], mine).astype(I32) + (256 * 512 + 256)
            owner, local = row >> 11, row & 2047
            member = rows_iota(128, 128) == owner
            member16 = member.astype(F32).astype(BF16)
            ahead = dot(member16, upper)
            rank = jnp.sum(
                jnp.where(member, ahead[:, :128] + carry[...], 0.0), axis=0, keepdims=True
            ).astype(I32)
            carry[...] += ahead[:, 128:]
            place_ref[pl.ds(b * BLOCK + j, 1), :] = owner * slots + rank
            mark = rows_iota(slots, 128) == rank
            code = ((b * BLOCK + j) * 128 + lanes_iota(1, 128)) * 2048 + local
            values.append(
                jnp.concatenate(
                    [
                        jnp.where(mark, piece.astype(F32), 0.0)
                        for piece in (code >> 18, ((code >> 9) & 511) - 256, (code & 511) - 256)
                    ],
                    axis=0,
                ).astype(BF16)
            )
            members.append(member16)
        acc[...] += lax.dot_general(
            jnp.concatenate(members, axis=1),
            jnp.concatenate(values, axis=1),
            NT,
            preferred_element_type=F32,
        )
        return 0

    lax.fori_loop(0, set_ref.shape[0] // BLOCK, block, 0)
    total = acc[...]
    first, second, third = (
        total[:, slots * p : slots * (p + 1)].astype(I32) for p in range(3)
    )
    code = (first << 18) + ((second + 256) << 9) + third + 256
    local, source = code & 2047, code >> 11
    for p in range(2):
        source_ref[pl.ds(p, devices, stride=2), :] = source[:, 128 * p : 128 * (p + 1)]
    index2 = set2_ref[...]
    home2 = home2_ref[...]
    marks2 = one_hot_rows(home2.shape[0], index2 >> 7)
    top2 = dot((home2 >> 7).astype(F32).T.astype(BF16), marks2)
    bottom2 = dot((home2 & 127).astype(F32).T.astype(BF16), marks2)
    mine2 = index2 & 127
    row2 = pick(top2, mine2).astype(I32) * 128 + pick(bottom2, mine2).astype(I32)
    owner2, local2 = row2 >> 6, row2 & 63
    member2 = rows_iota(128, 128) == owner2
    ahead2 = dot(member2.astype(F32).astype(BF16), upper)
    rank2 = jnp.sum(jnp.where(member2, ahead2[:, :128], 0.0), axis=0, keepdims=True).astype(I32)
    place2_ref[...] = owner2 * 2 + rank2
    value2 = jnp.where(rows_iota(slots, 128) == rank2, (local2 + 1).astype(F32), 0.0).astype(BF16)
    extra = lax.dot_general(
        member2.astype(F32).astype(BF16), value2, NT, preferred_element_type=F32
    )
    wanted = local + (extra.astype(I32) << 11)
    for p in range(2):
        want_ref[:, p, :] = wanted[:, 128 * p : 128 * (p + 1)]


def route(opp_set, opp_home, br_set, br_home, devices, slots):
    hist = opp_set.shape[0]
    return pl.pallas_call(
        route_kernel,
        out_shape=(
            jax.ShapeDtypeStruct((devices, 2, slots // 2), I32),
            jax.ShapeDtypeStruct((2 * devices, slots // 2), I32),
            jax.ShapeDtypeStruct((hist // 128, 128), I32),
            jax.ShapeDtypeStruct((1, 128), I32),
        ),
        scratch_shapes=[
            pltpu.VMEM((512, opp_home.shape[0] // 256), BF16),
            pltpu.VMEM((devices, 3 * slots), F32),
            pltpu.VMEM((devices, 128), F32),
        ],
        name="route",
    )(
        opp_set.reshape(-1, 128),
        opp_home.reshape(-1, 128),
        br_set.reshape(1, -1),
        br_home.reshape(-1, 128),
    )


def split(x):
    high = x.astype(BF16)
    return high, (x - high.astype(F32)).astype(BF16)


def find(pieces, rows, index, high_of, low_of):
    marks = jnp.concatenate(
        [one_hot_rows(rows, high_of(index[j : j + 1, :])) for j in range(BLOCK)], axis=1
    )
    both = dot(pieces, jnp.concatenate([marks, marks], axis=0))
    return [
        pick(both[:, 128 * j : 128 * (j + 1)], low_of(index[j : j + 1, :])) for j in range(BLOCK)
    ]


def look_up(pieces, rows, index_ref, out_ref, high_of, low_of, cast=lambda x: x, part=(0, 2)):
    def block(b, _):
        at = pl.ds(pl.multiple_of(b * BLOCK, BLOCK), BLOCK)
        for j, row in enumerate(find(pieces, rows, index_ref[at, :], high_of, low_of)):
            out_ref[pl.ds(b * BLOCK + j, 1), :] = cast(row)
        return 0

    half = index_ref.shape[0] // BLOCK // 2
    lax.fori_loop(part[0] * half, part[1] * half, block, 0)


def exchange_kernel(sizes, source_ref, want_ref, place_ref, next_ref, place2_ref, reach_ref,
                    cum_ref, br_ref, child_ref,
                    value_ref, gap_ref, total_ref,
                    asked, columns, table, wide, send, recv, gathered, sums, jump,
                    outgoing, incoming, part, parts_one, parts_two, middle_ref, ask_mid, act_mid,
                    child16, child_sem, ask_sems, row_out, row_in, act_sems, sum_sems):
    devices, slots, acts = send.shape
    me = [lax.axis_index(a) for a in AXES]

    def number(c):
        return ((c[0] * sizes[1] + c[1]) * sizes[2] + c[2]) * sizes[3] + c[3]

    my = number(me)

    def rem(x, n):
        return lax.rem(x, jnp.int32(n))

    def div(x, n):
        return lax.div(x, jnp.int32(n))

    def shift(i):
        q, s = div(i, 2), 2 * rem(i, 2)
        return (
            rem(q, 4) + s,
            rem(div(q, 32) + i, 2),
            rem(q + div(q, 4), 4) + s,
            rem(q + div(q, 16), 2) + s,
        )

    def to(i):
        c = tuple(rem(m + d, n) for m, d, n in zip(me, shift(i), sizes))
        return c, number(c)

    def back(i):
        return number(tuple(rem(m + 2 * n - d, n) for m, d, n in zip(me, shift(i), sizes)))

    def copy(src, dst, out_sem, in_sem, device):
        return pltpu.make_async_remote_copy(
            src_ref=src, dst_ref=dst, send_sem=out_sem, recv_sem=in_sem,
            device_id=device, device_id_type=pl.DeviceIdType.MESH,
        )

    def each(body, first=1):
        lax.fori_loop(first, devices, lambda i, c: (body(i), c)[1], 0)

    child_in = pltpu.make_async_copy(child_ref, child16, child_sem)
    child_in.start()
    barrier = pltpu.get_barrier_semaphore()
    each(lambda i: pl.semaphore_signal(
        barrier, inc=1, device_id=to(i)[0], device_id_type=pl.DeviceIdType.MESH))
    rows = table.shape[0]
    for p in range(4):
        cum = cum_ref[p * rows : (p + 1) * rows, :]
        policy = cum / jnp.sum(cum, axis=1, keepdims=True)
        table[:, 128 * p : 128 * (p + 1)] = policy.astype(BF16)
    places = place_ref[...]
    look_up(
        jnp.concatenate(
            [((places >> 8) * 256).astype(F32).astype(BF16), (places & 255).astype(F32).astype(BF16)],
            axis=1,
        ),
        128, next_ref, jump, lambda x: x & 127, lambda x: x >> 7, lambda x: x.astype(I32),
    )
    most = pl.ds(0, devices - 1)
    child_in.wait()
    wide[...] = child16[...].astype(F32)
    pl.semaphore_wait(barrier, devices - 1)

    first, second = me[0] * sizes[1] + me[1], me[2] * sizes[3] + me[3]
    near, far = sizes[0] * sizes[1], sizes[2] * sizes[3]

    def along_first(t):
        c = rem(me[0] + div(t, sizes[1]), sizes[0]), rem(me[1] + rem(t, sizes[1]), sizes[1])
        return (*c, me[2], me[3]), c[0] * sizes[1] + c[1]

    def along_second(t):
        c = rem(me[2] + div(t, sizes[3]), sizes[2]), rem(me[3] + rem(t, sizes[3]), sizes[3])
        return (me[0], me[1], *c), c[0] * sizes[3] + c[1]

    def over(count, body):
        lax.fori_loop(1, count, lambda t, c: (body(t), c)[1], 0)

    def stage_one(source, middle, sems):
        def go(t):
            device, n = along_first(t)
            copy(source.at[n], middle.at[first], sems.at[0], sems.at[1], device).start()

        over(near, go)
        middle[first] = source[first]

    def stage_two(middle, target, sems):
        some = pl.ds(0, near - 1)
        copy(middle.at[some], middle.at[some], sems.at[0], sems.at[1], tuple(me)).wait()

        def go(t):
            device, n = along_second(t)
            copy(middle.at[:, n], target.at[:, second], sems.at[2], sems.at[3], device).start()

        over(far, go)
        target[:, second] = middle[:, second]

    def stage_end(middle, target, sems):
        some = pl.ds(0, far - 1)
        copy(middle.at[:, some], target.at[:, some], sems.at[2], sems.at[3], tuple(me)).wait()

    most = pl.ds(0, devices - 1)
    stage_one(want_ref, ask_mid, ask_sems)
    stage_two(ask_mid, asked, ask_sems)
    stage_end(ask_mid, asked, ask_sems)
    for p in range(2):
        rowwise = asked[:, :, p, :].reshape(devices, 128)
        columns[128 * p : 128 * (p + 1), :] = rowwise.astype(F32).T.astype(I32)

    def served(n):
        column = jnp.sum(
            jnp.where(lanes_iota(slots, devices) == n, columns[...], 0), axis=1, keepdims=True
        ) & (4 * rows - 1)
        marks = (lanes_iota(slots, rows) == (column & (rows - 1))).astype(F32).astype(BF16)
        found = dot(marks, table[...])
        which = column // rows
        out = found[:, 384:]
        for p in range(3):
            out = jnp.where(which == p, found[:, 128 * p : 128 * (p + 1)], out)
        return out.astype(BF16)

    def launch(i):
        device, n = to(i)
        copy(send.at[n], recv.at[my], row_out, row_in.at[my], device).start()

    def serve(i):
        send[to(i)[1]] = served(to(i)[1])

        @pl.when(i > 1)
        def _():
            launch(i - 1)

    each(serve)
    launch(jnp.int32(devices - 1))
    recv[my] = served(my)

    def consume(n):
        def some(g, _):
            row, start = 2 * n + g, pl.multiple_of(g * 128, 128)
            for q in range(128):
                gathered[pl.ds(start + q, 1), :] = wide[pl.ds(source_ref[row, q], 1), :]
            return 0

        lax.fori_loop(0, 2, some, 0)

    def finish(n):
        product = recv[n].astype(F32) * gathered[...]
        total = jnp.sum(product, axis=1, keepdims=True)
        sums[...] = jnp.where(lanes_iota(slots, devices) == n, total, sums[...])

    sums[...] = jnp.zeros_like(sums)
    consume(my)
    finish(my)

    def take(i):
        n = back(i)
        consume(n)
        copy(send.at[n], recv.at[n], row_out, row_in.at[n], tuple(me)).wait_recv()
        finish(n)

    each(take)
    pieces = jnp.concatenate(split(sums[...]), axis=1)
    look_up(pieces, 128, jump, part, lambda x: x >> 8, lambda x: x & 255)
    reach = jnp.sum(
        jnp.where(rows_iota(128, 128) == lanes_iota(128, 128), reach_ref[...], 0.0),
        axis=1, keepdims=True,
    )
    weighted = part[...] * reach
    high, low = split(weighted)
    for s in range(2):
        marks = (rows_iota(devices, 128) * 2 + s == place2_ref[...]).astype(F32).astype(BF16)
        outgoing[:, :, s, :] = (dot(marks, high) + dot(marks, low)).reshape(near, far, acts)

    stage_one(outgoing, act_mid, act_sems)
    look_up(pieces, 128, place_ref, value_ref, lambda x: x >> 8, lambda x: x & 255, part=(0, 1))
    stage_two(act_mid, incoming, act_sems)
    look_up(pieces, 128, place_ref, value_ref, lambda x: x >> 8, lambda x: x & 255, part=(1, 2))
    stage_end(act_mid, incoming, act_sems)
    action = jnp.zeros((br_ref.shape[0], acts), F32)
    for s in range(2):
        owned = columns[s : s + 1, :] >> 11
        member = (rows_iota(br_ref.shape[0], devices) + 1 == owned).astype(F32).astype(BF16)
        high, low = split(incoming[:, :, s, :].reshape(devices, acts))
        action += dot(member, high) + dot(member, low)
    br = br_ref[...]
    br_policy = br / jnp.sum(br, axis=1, keepdims=True)
    gap = jnp.max(action, axis=1, keepdims=True) - jnp.sum(br_policy * action, axis=1, keepdims=True)
    across = jnp.where(rows_iota(gap.shape[0], 128) == lanes_iota(gap.shape[0], 128), gap, 0.0)
    gap_row = jnp.sum(across, axis=0, keepdims=True)
    gap_ref[...] = gap_row[:, : gap_ref.shape[1]]
    lane = lanes_iota(1, 128)
    both = jnp.where(
        lane == 0,
        jnp.sum(gap_row, axis=1, keepdims=True),
        jnp.where(lane == 1, jnp.sum(reach_ref[...], axis=1, keepdims=True), 0.0),
    )
    parts_one[first] = both
    total_ref[...] = both

    def tell_first(t):
        copy(total_ref, parts_one.at[first], sum_sems.at[0], sum_sems.at[1], along_first(t)[0]).start()

    over(near, tell_first)
    some = pl.ds(0, near - 1)
    copy(parts_one.at[some], parts_one.at[some], sum_sems.at[0], sum_sems.at[1], tuple(me)).wait()
    middle = jnp.sum(parts_one[:, 0, :], axis=0, keepdims=True)
    parts_two[second] = middle
    middle_ref[...] = middle

    def tell_second(t):
        copy(middle_ref, parts_two.at[second], sum_sems.at[2], sum_sems.at[3], along_second(t)[0]).start()

    over(far, tell_second)
    some = pl.ds(0, far - 1)
    copy(parts_two.at[some], parts_two.at[some], sum_sems.at[2], sum_sems.at[3], tuple(me)).wait()
    total = jnp.sum(parts_two[:, 0, :], axis=0, keepdims=True)
    top = jnp.sum(jnp.where(lane == 0, total, 0.0), axis=1, keepdims=True)
    bottom = jnp.sum(jnp.where(lane == 1, total, 0.0), axis=1, keepdims=True)
    total_ref[...] = jnp.broadcast_to(top / bottom, (1, 128))
    copy(send.at[most], recv.at[most], row_out, row_in.at[0], tuple(me)).wait_send()


def exchange(sizes, source, want, place, child_row, place2, reach, opp_cum, br_cum, child_value):
    devices, slots = want.shape[0], want.shape[1] * want.shape[2]
    hist, acts = child_value.shape
    rows = opp_cum.shape[0] // 4
    near, far = sizes[0] * sizes[1], sizes[2] * sizes[3]
    vmem, smem = pl.BlockSpec(memory_space=pltpu.VMEM), pl.BlockSpec(memory_space=pltpu.SMEM)
    dma = pltpu.SemaphoreType.DMA
    return pl.pallas_call(
        functools.partial(exchange_kernel, sizes),
        in_specs=[smem] + [vmem] * 7 + [pl.BlockSpec(memory_space=pl.ANY)],
        out_specs=[vmem] * 3,
        out_shape=(
            jax.ShapeDtypeStruct((hist // 128, 128), F32),
            jax.ShapeDtypeStruct((1, br_cum.shape[0]), F32),
            jax.ShapeDtypeStruct((1, 128), F32),
        ),
        scratch_shapes=[
            pltpu.VMEM((near, far, 2, 128), I32),
            pltpu.VMEM((slots, devices), I32),
            pltpu.VMEM((rows, 4 * acts), BF16),
            pltpu.VMEM((hist, acts), F32),
            pltpu.VMEM((devices, slots, acts), BF16),
            pltpu.VMEM((devices, slots, acts), BF16),
            pltpu.VMEM((slots, acts), F32),
            pltpu.VMEM((slots, devices), F32),
            pltpu.VMEM((128, 128), I32),
            pltpu.VMEM((near, far, 2, acts), F32),
            pltpu.VMEM((near, far, 2, acts), F32),
            pltpu.VMEM((128, 128), F32),
            pltpu.VMEM((near, 1, 128), F32),
            pltpu.VMEM((far, 1, 128), F32),
            pltpu.VMEM((1, 128), F32),
            pltpu.VMEM((near, far, 2, 128), I32),
            pltpu.VMEM((near, far, 2, acts), F32),
            pltpu.VMEM((hist, acts), BF16),
            dma, dma((4,)), dma, dma((devices,)), dma((4,)), dma((4,)),
        ],
        compiler_params=pltpu.CompilerParams(collective_id=0, has_side_effects=True),
        name="exchange",
    )(
        source,
        want.reshape(near, far, 2, 128),
        place,
        child_row.reshape(-1, 128),
        place2,
        reach.reshape(1, -1),
        opp_cum,
        br_cum,
        child_value,
    )


def local(child_value, child_row, opp_set, opp_home, opp_cum, reach, br_set, br_home, br_cum):
    sizes = tuple(lax.axis_size(a) for a in AXES)
    devices = lax.axis_size(AXES)
    slots = 2 * child_value.shape[0] // devices
    want, source, place, place2 = route(opp_set, opp_home, br_set, br_home, devices, slots)
    history_value, gap, ratio = exchange(
        sizes, source, want, place, child_row, place2, reach, opp_cum, br_cum, child_value
    )
    return history_value.reshape(-1), gap.reshape(-1), ratio[0, 0]


def solution(mesh):
    torus = Mesh(mesh.devices.reshape(4, 2, 4, 4), AXES)
    rows, flat = P(AXES, None), P(AXES)
    placed = (rows, rows, flat, P(), rows, flat, flat, P(), rows)
    return jax.shard_map(
        local, mesh=torus, in_specs=placed, out_specs=(flat, flat, P()), check_vma=False
    )
```

```python
import functools

import jax
import jax.numpy as jnp
from jax import lax
from jax.experimental import pallas as pl
from jax.experimental.pallas import tpu as pltpu
from jax.sharding import Mesh
from jax.sharding import PartitionSpec as P

AXES = ("gx_0", "gx_1", "gy_0", "gy_1")
F32, BF16, I32 = jnp.float32, jnp.bfloat16, jnp.int32
NT = (((1,), (1,)), ((), ()))


def rows_iota(rows, cols):
    return lax.broadcasted_iota(I32, (rows, cols), 0)


def lanes_iota(rows, cols):
    return lax.broadcasted_iota(I32, (rows, cols), 1)


def dot(a, b):
    return jnp.dot(a, b, preferred_element_type=F32)


def one_hot_rows(rows, index):
    return (rows_iota(rows, index.shape[1]) == index).astype(F32).astype(BF16)


def pick(table, index, base=0):
    rows, n = table.shape
    mark = rows_iota(rows, n) == index
    return jnp.sum(jnp.where(mark, table, 0.0), axis=0, keepdims=True)


BLOCK = 8


def route_kernel(set_ref, home_ref, set2_ref, home2_ref,
                 want_ref, source_ref, place_ref, place2_ref,
                 table, acc, carry):
    devices, slots = want_ref.shape[0], 256
    wide = table.shape[1] // 2
    for q in range(4):
        home = home_ref[pl.ds(q, wide, stride=4), :]
        lanes = slice(128 * q, 128 * (q + 1))
        table[lanes, :wide] = (((home >> 9) - 256) * 512).astype(F32).T.astype(BF16)
        table[lanes, wide:] = ((home & 511) - 256).astype(F32).T.astype(BF16)
    acc[...] = jnp.zeros_like(acc)
    carry[...] = jnp.zeros_like(carry)
    upper = jnp.concatenate(
        [(rows_iota(128, 128) < lanes_iota(128, 128)).astype(F32), jnp.ones((128, 128), F32)], axis=1
    ).astype(BF16)

    def block(b, _):
        at = pl.ds(pl.multiple_of(b * BLOCK, BLOCK), BLOCK)
        index = set_ref[at, :]
        high, low = index >> 9, index & 511
        each = BLOCK // 2
        marks = [
            jnp.concatenate(
                [one_hot_rows(wide, high[j : j + 1, :]) for j in range(h * each, (h + 1) * each)],
                axis=1,
            )
            for h in range(2)
        ]
        halves = [dot(table[...], jnp.concatenate([m, m], axis=0)) for m in marks]
        members, values = [], []
        for j in range(BLOCK):
            found, at_lane = halves[j // each], j % each
            lanes = slice(128 * at_lane, 128 * (at_lane + 1))
            mine = low[j : j + 1, :]
            row = pick(found[:, lanes], mine).astype(I32) + (256 * 512 + 256)
            owner, local = row >> 11, row & 2047
            member = rows_iota(128, 128) == owner
            member16 = member.astype(F32).astype(BF16)
            ahead = dot(member16, upper)
            rank = jnp.sum(
                jnp.where(member, ahead[:, :128] + carry[...], 0.0), axis=0, keepdims=True
            ).astype(I32)
            carry[...] += ahead[:, 128:]
            place_ref[pl.ds(b * BLOCK + j, 1), :] = owner * slots + rank
            mark = rows_iota(slots, 128) == rank
            code = ((b * BLOCK + j) * 128 + lanes_iota(1, 128)) * 2048 + local
            values.append(
                jnp.concatenate(
                    [
                        jnp.where(mark, piece.astype(F32), 0.0)
                        for piece in (code >> 18, ((code >> 9) & 511) - 256, (code & 511) - 256)
                    ],
                    axis=0,
                ).astype(BF16)
            )
            members.append(member16)
        acc[...] += lax.dot_general(
            jnp.concatenate(values, axis=1),
            jnp.concatenate(members, axis=1),
            NT,
            preferred_element_type=F32,
        )
        return 0

    lax.fori_loop(0, set_ref.shape[0] // BLOCK, block, 0)
    total = acc[...]
    first, second, third = (
        total[slots * p : slots * (p + 1), :].T.astype(I32) for p in range(3)
    )
    code = (first << 18) + ((second + 256) << 9) + third + 256
    local, source = code & 2047, code >> 11
    for p in range(2):
        source_ref[pl.ds(p, devices, stride=2), :] = source[:, 128 * p : 128 * (p + 1)]
    index2 = set2_ref[...]
    home2 = home2_ref[...]
    marks2 = one_hot_rows(home2.shape[0], index2 >> 7)
    top2 = dot((home2 >> 7).astype(F32).T.astype(BF16), marks2)
    bottom2 = dot((home2 & 127).astype(F32).T.astype(BF16), marks2)
    mine2 = index2 & 127
    row2 = pick(top2, mine2).astype(I32) * 128 + pick(bottom2, mine2).astype(I32)
    owner2, local2 = row2 >> 6, row2 & 63
    member2 = rows_iota(128, 128) == owner2
    ahead2 = dot(member2.astype(F32).astype(BF16), upper)
    rank2 = jnp.sum(jnp.where(member2, ahead2[:, :128], 0.0), axis=0, keepdims=True).astype(I32)
    place2_ref[...] = owner2 * 2 + rank2
    value2 = jnp.where(rows_iota(slots, 128) == rank2, (local2 + 1).astype(F32), 0.0).astype(BF16)
    extra = lax.dot_general(
        member2.astype(F32).astype(BF16), value2, NT, preferred_element_type=F32
    )
    wanted = local + (extra.astype(I32) << 11)
    for p in range(2):
        want_ref[:, p, :] = wanted[:, 128 * p : 128 * (p + 1)]


def route(opp_set, opp_home, br_set, br_home, devices, slots):
    hist = opp_set.shape[0]
    return pl.pallas_call(
        route_kernel,
        out_shape=(
            jax.ShapeDtypeStruct((devices, 2, slots // 2), I32),
            jax.ShapeDtypeStruct((2 * devices, slots // 2), I32),
            jax.ShapeDtypeStruct((hist // 128, 128), I32),
            jax.ShapeDtypeStruct((1, 128), I32),
        ),
        scratch_shapes=[
            pltpu.VMEM((512, opp_home.shape[0] // 256), BF16),
            pltpu.VMEM((3 * slots, devices), F32),
            pltpu.VMEM((devices, 128), F32),
        ],
        name="route",
    )(
        opp_set.reshape(-1, 128),
        opp_home.reshape(-1, 128),
        br_set.reshape(1, -1),
        br_home.reshape(-1, 128),
    )


def split(x):
    high = x.astype(BF16)
    return high, (x - high.astype(F32)).astype(BF16)


def find(pieces, rows, index, high_of, low_of):
    marks = jnp.concatenate(
        [one_hot_rows(rows, high_of(index[j : j + 1, :])) for j in range(BLOCK)], axis=1
    )
    both = dot(pieces, jnp.concatenate([marks, marks], axis=0))
    return [
        pick(both[:, 128 * j : 128 * (j + 1)], low_of(index[j : j + 1, :])) for j in range(BLOCK)
    ]


def look_up(pieces, rows, index_ref, out_ref, high_of, low_of, cast=lambda x: x, part=(0, 2)):
    def block(b, _):
        at = pl.ds(pl.multiple_of(b * BLOCK, BLOCK), BLOCK)
        for j, row in enumerate(find(pieces, rows, index_ref[at, :], high_of, low_of)):
            out_ref[pl.ds(b * BLOCK + j, 1), :] = cast(row)
        return 0

    half = index_ref.shape[0] // BLOCK // 2
    lax.fori_loop(part[0] * half, part[1] * half, block, 0)


def exchange_kernel(sizes, source_ref, want_ref, place_ref, next_ref, place2_ref, reach_ref,
                    cum_ref, br_ref, child_ref,
                    value_ref, gap_ref, total_ref,
                    asked, columns, table, wide, send, recv, gathered, sums, jump,
                    outgoing, incoming, part, parts_one, parts_two, middle_ref, ask_mid, act_mid,
                    child16, child_sem, ask_sems, row_out, row_in, act_sems, sum_sems):
    devices, slots, acts = send.shape
    me = [lax.axis_index(a) for a in AXES]

    def number(c):
        return ((c[0] * sizes[1] + c[1]) * sizes[2] + c[2]) * sizes[3] + c[3]

    my = number(me)

    def rem(x, n):
        return lax.rem(x, jnp.int32(n))

    def div(x, n):
        return lax.div(x, jnp.int32(n))

    def shift(i):
        q, s = div(i, 2), 2 * rem(i, 2)
        return (
            rem(q, 4) + s,
            rem(div(q, 32) + i, 2),
            rem(q + div(q, 4), 4) + s,
            rem(q + div(q, 16), 2) + s,
        )

    def to(i):
        c = tuple(rem(m + d, n) for m, d, n in zip(me, shift(i), sizes))
        return c, number(c)

    def back(i):
        return number(tuple(rem(m + 2 * n - d, n) for m, d, n in zip(me, shift(i), sizes)))

    def copy(src, dst, out_sem, in_sem, device):
        return pltpu.make_async_remote_copy(
            src_ref=src, dst_ref=dst, send_sem=out_sem, recv_sem=in_sem,
            device_id=device, device_id_type=pl.DeviceIdType.MESH,
        )

    def each(body, first=1):
        lax.fori_loop(first, devices, lambda i, c: (body(i), c)[1], 0)

    child_in = pltpu.make_async_copy(child_ref, child16, child_sem)
    child_in.start()
    barrier = pltpu.get_barrier_semaphore()
    each(lambda i: pl.semaphore_signal(
        barrier, inc=1, device_id=to(i)[0], device_id_type=pl.DeviceIdType.MESH))
    rows = table.shape[0]
    for p in range(4):
        cum = cum_ref[p * rows : (p + 1) * rows, :]
        policy = cum / jnp.sum(cum, axis=1, keepdims=True)
        table[:, 128 * p : 128 * (p + 1)] = policy.astype(BF16)
    places = place_ref[...]
    look_up(
        jnp.concatenate(
            [((places >> 8) * 256).astype(F32).astype(BF16), (places & 255).astype(F32).astype(BF16)],
            axis=1,
        ),
        128, next_ref, jump, lambda x: x & 127, lambda x: x >> 7, lambda x: x.astype(I32),
    )
    most = pl.ds(0, devices - 1)
    child_in.wait()
    wide[...] = child16[...].astype(F32)
    pl.semaphore_wait(barrier, devices - 1)

    first, second = me[0] * sizes[1] + me[1], me[2] * sizes[3] + me[3]
    near, far = sizes[0] * sizes[1], sizes[2] * sizes[3]

    def along_first(t):
        c = rem(me[0] + div(t, sizes[1]), sizes[0]), rem(me[1] + rem(t, sizes[1]), sizes[1])
        return (*c, me[2], me[3]), c[0] * sizes[1] + c[1]

    def along_second(t):
        c = rem(me[2] + div(t, sizes[3]), sizes[2]), rem(me[3] + rem(t, sizes[3]), sizes[3])
        return (me[0], me[1], *c), c[0] * sizes[3] + c[1]

    def over(count, body):
        lax.fori_loop(1, count, lambda t, c: (body(t), c)[1], 0)

    def stage_one(source, middle, sems):
        def go(t):
            device, n = along_first(t)
            copy(source.at[n], middle.at[first], sems.at[0], sems.at[1], device).start()

        over(near, go)
        middle[first] = source[first]

    def stage_two(middle, target, sems):
        some = pl.ds(0, near - 1)
        copy(middle.at[some], middle.at[some], sems.at[0], sems.at[1], tuple(me)).wait()

        def go(t):
            device, n = along_second(t)
            copy(middle.at[:, n], target.at[:, second], sems.at[2], sems.at[3], device).start()

        over(far, go)
        target[:, second] = middle[:, second]

    def stage_end(middle, target, sems):
        some = pl.ds(0, far - 1)
        copy(middle.at[:, some], target.at[:, some], sems.at[2], sems.at[3], tuple(me)).wait()

    most = pl.ds(0, devices - 1)
    stage_one(want_ref, ask_mid, ask_sems)
    stage_two(ask_mid, asked, ask_sems)
    stage_end(ask_mid, asked, ask_sems)
    for p in range(2):
        rowwise = asked[:, :, p, :].reshape(devices, 128)
        columns[128 * p : 128 * (p + 1), :] = rowwise.astype(F32).T.astype(I32)

    def served(n):
        column = jnp.sum(
            jnp.where(lanes_iota(slots, devices) == n, columns[...], 0), axis=1, keepdims=True
        ) & (4 * rows - 1)
        marks = (lanes_iota(slots, rows) == (column & (rows - 1))).astype(F32).astype(BF16)
        found = dot(marks, table[...])
        which = column // rows
        out = found[:, 384:]
        for p in range(3):
            out = jnp.where(which == p, found[:, 128 * p : 128 * (p + 1)], out)
        return out.astype(BF16)

    def launch(i):
        device, n = to(i)
        copy(send.at[n], recv.at[my], row_out, row_in.at[my], device).start()

    def serve(i):
        send[to(i)[1]] = served(to(i)[1])

        @pl.when(i > 1)
        def _():
            launch(i - 1)

    each(serve)
    launch(jnp.int32(devices - 1))
    recv[my] = served(my)

    def consume(n):
        def some(g, _):
            row, start = 2 * n + g, pl.multiple_of(g * 128, 128)
            for q in range(128):
                gathered[pl.ds(start + q, 1), :] = wide[pl.ds(source_ref[row, q], 1), :]
            return 0

        lax.fori_loop(0, 2, some, 0)

    def finish(n):
        product = recv[n].astype(F32) * gathered[...]
        total = jnp.sum(product, axis=1, keepdims=True)
        sums[...] = jnp.where(lanes_iota(slots, devices) == n, total, sums[...])

    sums[...] = jnp.zeros_like(sums)
    consume(my)
    finish(my)

    def take(i):
        n = back(i)
        consume(n)
        copy(send.at[n], recv.at[n], row_out, row_in.at[n], tuple(me)).wait_recv()
        finish(n)

    each(take)
    pieces = jnp.concatenate(split(sums[...]), axis=1)
    look_up(pieces, 128, jump, part, lambda x: x >> 8, lambda x: x & 255)
    reach = jnp.sum(
        jnp.where(rows_iota(128, 128) == lanes_iota(128, 128), reach_ref[...], 0.0),
        axis=1, keepdims=True,
    )
    weighted = part[...] * reach
    high, low = split(weighted)
    for s in range(2):
        marks = (rows_iota(devices, 128) * 2 + s == place2_ref[...]).astype(F32).astype(BF16)
        outgoing[:, :, s, :] = (dot(marks, high) + dot(marks, low)).reshape(near, far, acts)

    stage_one(outgoing, act_mid, act_sems)
    look_up(pieces, 128, place_ref, value_ref, lambda x: x >> 8, lambda x: x & 255, part=(0, 1))
    stage_two(act_mid, incoming, act_sems)
    look_up(pieces, 128, place_ref, value_ref, lambda x: x >> 8, lambda x: x & 255, part=(1, 2))
    stage_end(act_mid, incoming, act_sems)
    action = jnp.zeros((br_ref.shape[0], acts), F32)
    for s in range(2):
        owned = columns[s : s + 1, :] >> 11
        member = (rows_iota(br_ref.shape[0], devices) + 1 == owned).astype(F32).astype(BF16)
        high, low = split(incoming[:, :, s, :].reshape(devices, acts))
        action += dot(member, high) + dot(member, low)
    br = br_ref[...]
    br_policy = br / jnp.sum(br, axis=1, keepdims=True)
    gap = jnp.max(action, axis=1, keepdims=True) - jnp.sum(br_policy * action, axis=1, keepdims=True)
    across = jnp.where(rows_iota(gap.shape[0], 128) == lanes_iota(gap.shape[0], 128), gap, 0.0)
    gap_row = jnp.sum(across, axis=0, keepdims=True)
    gap_ref[...] = gap_row[:, : gap_ref.shape[1]]
    lane = lanes_iota(1, 128)
    both = jnp.where(
        lane == 0,
        jnp.sum(gap_row, axis=1, keepdims=True),
        jnp.where(lane == 1, jnp.sum(reach_ref[...], axis=1, keepdims=True), 0.0),
    )
    parts_one[first] = both
    total_ref[...] = both

    def tell_first(t):
        copy(total_ref, parts_one.at[first], sum_sems.at[0], sum_sems.at[1], along_first(t)[0]).start()

    over(near, tell_first)
    some = pl.ds(0, near - 1)
    copy(parts_one.at[some], parts_one.at[some], sum_sems.at[0], sum_sems.at[1], tuple(me)).wait()
    middle = jnp.sum(parts_one[:, 0, :], axis=0, keepdims=True)
    parts_two[second] = middle
    middle_ref[...] = middle

    def tell_second(t):
        copy(middle_ref, parts_two.at[second], sum_sems.at[2], sum_sems.at[3], along_second(t)[0]).start()

    over(far, tell_second)
    some = pl.ds(0, far - 1)
    copy(parts_two.at[some], parts_two.at[some], sum_sems.at[2], sum_sems.at[3], tuple(me)).wait()
    total = jnp.sum(parts_two[:, 0, :], axis=0, keepdims=True)
    top = jnp.sum(jnp.where(lane == 0, total, 0.0), axis=1, keepdims=True)
    bottom = jnp.sum(jnp.where(lane == 1, total, 0.0), axis=1, keepdims=True)
    total_ref[...] = jnp.broadcast_to(top / bottom, (1, 128))
    copy(send.at[most], recv.at[most], row_out, row_in.at[0], tuple(me)).wait_send()


def exchange(sizes, source, want, place, child_row, place2, reach, opp_cum, br_cum, child_value):
    devices, slots = want.shape[0], want.shape[1] * want.shape[2]
    hist, acts = child_value.shape
    rows = opp_cum.shape[0] // 4
    near, far = sizes[0] * sizes[1], sizes[2] * sizes[3]
    vmem, smem = pl.BlockSpec(memory_space=pltpu.VMEM), pl.BlockSpec(memory_space=pltpu.SMEM)
    dma = pltpu.SemaphoreType.DMA
    return pl.pallas_call(
        functools.partial(exchange_kernel, sizes),
        in_specs=[smem] + [vmem] * 7 + [pl.BlockSpec(memory_space=pl.ANY)],
        out_specs=[vmem] * 3,
        out_shape=(
            jax.ShapeDtypeStruct((hist // 128, 128), F32),
            jax.ShapeDtypeStruct((1, br_cum.shape[0]), F32),
            jax.ShapeDtypeStruct((1, 128), F32),
        ),
        scratch_shapes=[
            pltpu.VMEM((near, far, 2, 128), I32),
            pltpu.VMEM((slots, devices), I32),
            pltpu.VMEM((rows, 4 * acts), BF16),
            pltpu.VMEM((hist, acts), F32),
            pltpu.VMEM((devices, slots, acts), BF16),
            pltpu.VMEM((devices, slots, acts), BF16),
            pltpu.VMEM((slots, acts), F32),
            pltpu.VMEM((slots, devices), F32),
            pltpu.VMEM((128, 128), I32),
            pltpu.VMEM((near, far, 2, acts), F32),
            pltpu.VMEM((near, far, 2, acts), F32),
            pltpu.VMEM((128, 128), F32),
            pltpu.VMEM((near, 1, 128), F32),
            pltpu.VMEM((far, 1, 128), F32),
            pltpu.VMEM((1, 128), F32),
            pltpu.VMEM((near, far, 2, 128), I32),
            pltpu.VMEM((near, far, 2, acts), F32),
            pltpu.VMEM((hist, acts), BF16),
            dma, dma((4,)), dma, dma((devices,)), dma((4,)), dma((4,)),
        ],
        compiler_params=pltpu.CompilerParams(collective_id=0, has_side_effects=True),
        name="exchange",
    )(
        source,
        want.reshape(near, far, 2, 128),
        place,
        child_row.reshape(-1, 128),
        place2,
        reach.reshape(1, -1),
        opp_cum,
        br_cum,
        child_value,
    )


def local(child_value, child_row, opp_set, opp_home, opp_cum, reach, br_set, br_home, br_cum):
    sizes = tuple(lax.axis_size(a) for a in AXES)
    devices = lax.axis_size(AXES)
    slots = 2 * child_value.shape[0] // devices
    want, source, place, place2 = route(opp_set, opp_home, br_set, br_home, devices, slots)
    history_value, gap, ratio = exchange(
        sizes, source, want, place, child_row, place2, reach, opp_cum, br_cum, child_value
    )
    return history_value.reshape(-1), gap.reshape(-1), ratio[0, 0]


def solution(mesh):
    torus = Mesh(mesh.devices.reshape(4, 2, 4, 4), AXES)
    rows, flat = P(AXES, None), P(AXES)
    placed = (rows, rows, flat, P(), rows, flat, flat, P(), rows)
    return jax.shard_map(
        local, mesh=torus, in_specs=placed, out_specs=(flat, flat, P()), check_vma=False
    )
```
